32 devices in a mesh: context: 4 (over y, x), experts: 8 (over z, core).
Axes of the slice: x: 2, y: 2, z: 4, core: 2. Of those that a mesh axis runs over, the one named last changes fastest.
Arguments:
- inputs: bfloat16 [8, 512, 2048], P('experts', 'context'), may hold values from -6 to 6
- cotangent: bfloat16 [8, 512, 2048], P('experts', 'context'), may hold values from -6 to 6
- expert_ids: int32 [8, 512, 6], P('experts', 'context'), may hold values from 0 to 15, all different within a row; in each aligned block of 128 rows (0 to 127, 128 to 255, ..., all dimensions but the last counted through in order) at most 56 rows name the same one
- attn_gain: bfloat16 [2048], P(('context', 'experts')), may hold values from 0.5 to 1.5
- query_weight: bfloat16 [2048, 3072], P(('context', 'experts')), may hold values from -0.125 to 0.125
- latent_down: bfloat16 [2048, 576], P(('context', 'experts')), may hold values from -0.125 to 0.125
- latent_gain: bfloat16 [512], P(('context', 'experts')), may hold values from 0.5 to 1.5
- latent_up: bfloat16 [512, 4096], P(('context', 'experts')), may hold values from -0.25 to 0.25
- output_weight: bfloat16 [2048, 2048], P(('context', 'experts')), may hold values from -1.5 to 1.5
- ffn_gain: bfloat16 [2048], P(('context', 'experts')), may hold values from 0.5 to 1.5
- router_weight: bfloat16 [2048, 16], P(('context', 'experts')), may hold values from -0.0625 to 0.0625
- shared_gate: bfloat16 [2048, 2816], P(('context', 'experts')), may hold values from -0.125 to 0.125
- shared_up: bfloat16 [2048, 2816], P(('context', 'experts')), may hold values from -0.125 to 0.125
- shared_down: bfloat16 [2816, 2048], P(('context', 'experts')), may hold values from -0.109375 to 0.109375
- expert_gate: bfloat16 [16, 2048, 1408], P('experts', None, 'context'), may hold values from -0.125 to 0.125
- expert_up: bfloat16 [16, 2048, 1408], P('experts', None, 'context'), may hold values from -0.125 to 0.125
- expert_down: bfloat16 [16, 1408, 2048], P('experts', 'context'), may hold values from -6 to 6
Outputs:
- output: bfloat16 [8, 512, 2048], P('experts', 'context')
- inputs_grad: float32 [8, 512, 2048], P('experts', 'context')
- attn_gain_grad: float32 [2048], P(('context', 'experts'))
- query_weight_grad: float32 [2048, 3072], P(('context', 'experts'))
- latent_down_grad: float32 [2048, 576], P(('context', 'experts'))
- latent_gain_grad: float32 [512], P(('context', 'experts'))
- latent_up_grad: float32 [512, 4096], P(('context', 'experts'))
- output_weight_grad: float32 [2048, 2048], P(('context', 'experts'))
- ffn_gain_grad: float32 [2048], P(('context', 'experts'))
- router_weight_grad: float32 [2048, 16], P(('context', 'experts'))
- shared_gate_grad: float32 [2048, 2816], P(('context', 'experts'))
- shared_up_grad: float32 [2048, 2816], P(('context', 'experts'))
- shared_down_grad: float32 [2816, 2048], P(('context', 'experts'))
- expert_gate_grad: float32 [16, 2048, 1408], P('experts', None, 'context')
- expert_up_grad: float32 [16, 2048, 1408], P('experts', None, 'context')
- expert_down_grad: float32 [16, 1408, 2048], P('experts', 'context')
The draws below stay inside these ranges and needn't reach their ends.
Inputs may be any that keep to these rules, and one draw needn't show every extreme that they name: `expert_ids`: each token names 6 different experts. Among the 128 tokens of one device no expert is named more than 56 times, and in some such block one expert is named exactly 56 times.
All inputs are finite; a program needn't handle non-finite values.
Results may differ from the reference program's by a relative error of at most 0.024.
Values may be sent and summed in bfloat16 or wider, within the bound.
No kernel may reach another device: no remote copies, remote signals or barrier semaphores. Data moves between devices by JAX's collectives and lax.ppermute only.
A program may use at most 448 MiB of HBM per device.

```python
import math
import jax
import jax.numpy as jnp
import numpy as np
from jax import lax

D = 2048
HEADS = 16
NOPE = 128
ROPE_D = 64
VD = 128
KVR = 512
FF = 1408
SFF = 2816
TOP = 6
P_DEV = 64
C_DEV = 64
QK = 192
TOK_DEV = 128
PROMPT = 256
SEG = 512
GROUPS = 8
EXPERTS = 16
CAP = 56
N_CONTEXT = 4
N_EXPERTS = 8


def level_of(key, extent, split, least, top_value):
    def one(dim, parts):
        steps = jax.random.uniform(jax.random.fold_in(jax.random.fold_in(key, 6), dim), (parts,), jnp.float32, least / len(split), top_value / len(split))
        return jnp.repeat(jnp.exp(steps), extent[dim] // parts).reshape((-1,) + (1,) * (len(extent) - dim - 1))

    level = one(*split[0])
    for cut in split[1:]:
        level = level * one(*cut)
    return level


def assign_block(own_key, own, number, rows, amount, top, most, lean):
    sequence = jax.random.permutation(own_key, amount)
    packed, common = load_shares(amount, rows * top, most, lean, True), load_shares(amount, rows * top, most, lean, False)
    places = jnp.arange(amount)

    def named(lengths, turn):
        used = int((lengths > 0).sum())
        fixed = max(1, used // 4)
        moved = fixed + (places - fixed + turn * (used - fixed)) % max(1, amount - fixed)
        return jnp.zeros((amount,), jnp.int32).at[sequence[jnp.where(places < fixed, places, moved)]].set(jnp.asarray(lengths, jnp.int32))

    lengths = jnp.where(number % 4 == 0, named(packed, number // 4), named(common, number - number // 4 - 1))
    mixed = jax.random.permutation(jax.random.fold_in(own, 3), amount)
    giver, sink = mixed[0:amount // 2 * 2:2], mixed[1:amount // 2 * 2:2]
    room = jnp.minimum(lengths[giver] - 1, most - lengths[sink]) // 2
    room = jnp.where((giver == sequence[0]) | (sink == sequence[0]) | (lengths[sink] == 0), 0, jnp.maximum(room, 0))
    moved = jax.random.randint(jax.random.fold_in(own, 4), (amount // 2,), 0, 1 << 20) % (room + 1)
    lengths = lengths.at[giver].add(-moved).at[sink].add(moved)
    items = jnp.searchsorted(jnp.cumsum(lengths), jnp.arange(rows * top), side="right").astype(jnp.int32)
    grid = items.reshape(top, rows).T
    grid = grid[jax.random.permutation(jax.random.fold_in(own, 1), rows)]
    turn = jax.random.randint(jax.random.fold_in(own, 2), (rows, 1), 0, top)
    return jnp.take_along_axis(grid, (jnp.arange(top)[None, :] + turn) % top, axis=1)


def load_shares(amount, total, most, lean, full):
    weights = [(1 << 20) // math.isqrt(grade ** lean) + 1 for grade in range(1, amount + 1)]
    largest = most if full else min(most, max(-(-total // amount), total * weights[0] // sum(weights)))
    least = 1 if total - largest >= amount - 1 else 0
    given, surplus = [largest] + [least] * (amount - 1), total - largest - least * (amount - 1)
    while surplus > 0:
        movable = [i for i in range(1, amount) if given[i] < largest] or [i for i in range(1, amount) if given[i] < most]
        mass, budget = sum([weights[i] for i in movable]), surplus
        for i in movable:
            addition = min(most - given[i], max(1, budget * weights[i] // mass), surplus)
            given[i] = given[i] + addition
            surplus = surplus - addition
    return np.array(given)


def scatter_about(own_key, dims, scale, reach, cuts=(), dtype=jnp.bfloat16):
    values = jax.random.normal(own_key, dims, jnp.float32) * scale
    if len(cuts) > 0:
        values = level_of(own_key, dims, cuts, -0.22, 0.18) * values
    return jnp.clip(values, min=-reach, max=reach).astype(dtype)


def setup_inputs(seed: int = 0) -> dict:
    key_list = jax.random.split(jax.random.key(seed), 18)
    inputs = scatter_about(key_list[0], (GROUPS, SEG, D), 1.0, 6.0, ((0, 8), (1, 4)))
    cotangent = scatter_about(key_list[1], (GROUPS, SEG, D), 1.0, 6.0, ((0, 8), (1, 4)))
    expert_ids_keys = jax.random.split(jax.random.fold_in(key_list[2], 1), GROUPS * SEG // TOK_DEV)
    expert_ids_turns = jax.random.permutation(jax.random.fold_in(key_list[2], 3), GROUPS * SEG // TOK_DEV)
    expert_ids = jax.vmap(lambda own, number: assign_block(jax.random.fold_in(key_list[2], 2), own, number, TOK_DEV, EXPERTS, TOP, CAP, 1))(expert_ids_keys, expert_ids_turns).reshape((GROUPS, SEG, TOP))
    attn_gain = jnp.clip(1.0 + 0.1 * jax.random.normal(key_list[3], (D,), jnp.float32), 0.5, 1.5).astype(jnp.bfloat16)
    query_weight = scatter_about(key_list[4], (D, HEADS * QK), D ** -0.5, 0.125, ((0, 32),))
    latent_down = scatter_about(key_list[5], (D, KVR + ROPE_D), D ** -0.5, 0.125, ((0, 32),))
    latent_gain = jnp.clip(1.0 + 0.1 * jax.random.normal(key_list[6], (KVR,), jnp.float32), 0.5, 1.5).astype(jnp.bfloat16)
    latent_up = scatter_about(key_list[7], (KVR, HEADS * (NOPE + VD)), KVR ** -0.5, 0.25, ((0, 32),))
    output_weight = scatter_about(key_list[8], (HEADS * VD, D), (HEADS * VD // 128) ** -0.5, 1.5, ((0, 32),))
    ffn_gain = jnp.clip(1.0 + 0.1 * jax.random.normal(key_list[9], (D,), jnp.float32), 0.5, 1.5).astype(jnp.bfloat16)
    router_weight = scatter_about(key_list[10], (D, EXPERTS), (4 * D) ** -0.5, 0.0625, ((0, 32),))
    shared_gate = scatter_about(key_list[11], (D, SFF), D ** -0.5, 0.125, ((0, 32),))
    shared_up = scatter_about(key_list[12], (D, SFF), D ** -0.5, 0.125, ((0, 32),))
    shared_down = scatter_about(key_list[13], (SFF, D), SFF ** -0.5, 0.109375, ((0, 32),))
    expert_gate = scatter_about(key_list[14], (EXPERTS, D, FF), D ** -0.5, 0.125, ((0, 8), (2, 4)))
    expert_up = scatter_about(key_list[15], (EXPERTS, D, FF), D ** -0.5, 0.125, ((0, 8), (2, 4)))
    expert_down = scatter_about(key_list[16], (EXPERTS, FF, D), 1 ** -0.5, 6.0, ((0, 8), (1, 4)))
    return dict(inputs=inputs, cotangent=cotangent, expert_ids=expert_ids, attn_gain=attn_gain, query_weight=query_weight, latent_down=latent_down, latent_gain=latent_gain, latent_up=latent_up, output_weight=output_weight, ffn_gain=ffn_gain, router_weight=router_weight, shared_gate=shared_gate, shared_up=shared_up, shared_down=shared_down, expert_gate=expert_gate, expert_up=expert_up, expert_down=expert_down)


eps = 1e-06
highest = lax.Precision.HIGHEST

@jax.custom_vjp
def low(v):
    return lax.optimization_barrier(v.astype(jnp.bfloat16)).astype(jnp.float32)

@jax.custom_vjp
def low_back(v):
    return v

def low_keep(v):
    return (low(v), None)

def low_pass(kept, grad):
    return (grad,)

def back_keep(v):
    return (v, None)

def back_low(kept, grad):
    return (low(grad),)
low.defvjp(low_keep, low_pass)
low_back.defvjp(back_keep, back_low)

def matmul(left, right):
    return jnp.dot(left, right, precision=highest, preferred_element_type=jnp.float32)

def rotation(position, width):
    half = width // 2
    freqs = 10000.0 ** (-2.0 * jnp.arange(half).astype(jnp.float32) / width)
    angle = position.astype(jnp.float32)[:, None] * freqs[None, :]
    return (jnp.cos(angle), jnp.sin(angle))

def rotate(values, cosine, sine):
    half = values.shape[-1] // 2
    first = values[..., :half]
    second = values[..., half:]
    return jnp.concatenate([first * cosine - second * sine, first * sine + second * cosine], axis=-1)

def expert_rows(operands):
    rows, gate_w, up_w, down_w = operands
    gate_activation = low_back(matmul(rows, gate_w))
    up_activation = low_back(matmul(rows, up_w))
    return matmul(low(jax.nn.silu(gate_activation) * up_activation), down_w)

def layer(expert_ids, tokens, attn_gain, query_weight, latent_down, latent_gain, latent_up, output_weight, ffn_gain, router_weight, shared_gate, shared_up, shared_down, expert_gate, expert_up, expert_down):
    rows = jnp.arange(SEG)
    device = rows // TOK_DEV
    offset = rows % TOK_DEV
    place = jnp.where(offset < P_DEV, device * P_DEV + offset, PROMPT + device * C_DEV + offset - P_DEV)
    cosine, sine = rotation(place, ROPE_D)
    allowed = place[None, :] <= place[:, None]
    scale = 1.0 / math.sqrt(NOPE + ROPE_D)

    def attend(group):
        inv_root = lax.rsqrt(lax.optimization_barrier(jnp.mean(group * group, -1, keepdims=True)) + eps)
        normed = low(group * inv_root * attn_gain)
        query_raw = low_back(matmul(normed, query_weight)).reshape(SEG, HEADS, NOPE + ROPE_D)
        query_rot = low(jnp.concatenate([query_raw[..., :NOPE], rotate(query_raw[..., NOPE:], cosine[:, None, :], sine[:, None, :])], -1))
        latent_raw = low_back(matmul(normed, latent_down))
        compressed = latent_raw[:, :KVR]
        latent_norm = low(compressed * lax.rsqrt(lax.optimization_barrier(jnp.mean(compressed * compressed, -1, keepdims=True)) + eps) * latent_gain)
        key_rope = low(rotate(latent_raw[:, KVR:], cosine, sine))
        key_value = low(low_back(matmul(latent_norm, latent_up))).reshape(SEG, HEADS, NOPE + VD)
        keys_full = jnp.concatenate([key_value[..., :NOPE], jnp.broadcast_to(key_rope[:, None, :], (SEG, HEADS, ROPE_D))], -1)
        scores = low_back(jnp.einsum('thd,shd->hts', query_rot, keys_full, precision=highest, preferred_element_type=jnp.float32) * scale)
        scores = jnp.where(allowed[None], scores, -1e+30)
        row_peak = lax.optimization_barrier(jnp.max(scores, -1, keepdims=True))
        exp_scores = jnp.exp(scores - row_peak)
        weights = low(exp_scores / lax.optimization_barrier(jnp.sum(exp_scores, -1, keepdims=True)))
        attended = low_back(low(jnp.einsum('hts,shd->thd', weights, key_value[..., NOPE:], precision=highest, preferred_element_type=jnp.float32))).reshape(SEG, HEADS * VD)
        return group + low_back(matmul(attended, output_weight))
    hidden = lax.map(jax.checkpoint(attend), tokens).reshape(-1, D)
    count = hidden.shape[0]
    inv_mid = lax.rsqrt(lax.optimization_barrier(jnp.mean(hidden * hidden, -1, keepdims=True)) + eps)
    mixed = low(hidden * inv_mid * ffn_gain)
    logits = low_back(matmul(mixed, router_weight))
    router_probs = jax.nn.softmax(logits, axis=-1)
    chosen = expert_ids.reshape(count, TOP)
    gates = jnp.take_along_axis(router_probs, chosen, axis=1)
    shared_gval = low_back(matmul(mixed, shared_gate))
    shared_uval = low_back(matmul(mixed, shared_up))
    shared_out = matmul(low(jax.nn.silu(shared_gval) * shared_uval), shared_down)
    flat_ids = chosen.reshape(-1)
    id_hot = (flat_ids[:, None] == jnp.arange(EXPERTS)[None, :]).astype(jnp.int32)
    slot_rank = lax.optimization_barrier(jnp.sum((jnp.cumsum(id_hot, 0) - 1) * id_hot, 1))
    capacity = N_CONTEXT * N_EXPERTS * CAP
    slot_index = (flat_ids * capacity + slot_rank).astype(jnp.int32)
    sent = low_back(jnp.repeat(mixed, TOP, axis=0))
    buffer = jnp.zeros((EXPERTS * capacity, D), jnp.float32).at[slot_index].add(sent).reshape(EXPERTS, capacity, D)
    produced = lax.map(jax.checkpoint(expert_rows), (buffer, expert_gate, expert_up, expert_down))
    returned = low(low_back(produced)).reshape(EXPERTS * capacity, D)[slot_index].reshape(count, TOP, D)
    output = hidden + shared_out + lax.optimization_barrier(jnp.sum(gates[:, :, None] * returned, 1))
    return output.reshape(tokens.shape)

def reference(inputs, cotangent, expert_ids, attn_gain, query_weight, latent_down, latent_gain, latent_up, output_weight, ffn_gain, router_weight, shared_gate, shared_up, shared_down, expert_gate, expert_up, expert_down):
    floats = (inputs.astype(jnp.float32), attn_gain.astype(jnp.float32), query_weight.astype(jnp.float32), latent_down.astype(jnp.float32), latent_gain.astype(jnp.float32), latent_up.astype(jnp.float32), output_weight.astype(jnp.float32), ffn_gain.astype(jnp.float32), router_weight.astype(jnp.float32), shared_gate.astype(jnp.float32), shared_up.astype(jnp.float32), shared_down.astype(jnp.float32), expert_gate.astype(jnp.float32), expert_up.astype(jnp.float32), expert_down.astype(jnp.float32))

    def forward(*values):
        return layer(expert_ids, *values)
    output, pullback = jax.vjp(forward, *floats)
    grads = pullback(cotangent.astype(jnp.float32))
    return (output.astype(jnp.bfloat16), grads[0], grads[1], grads[2], grads[3], grads[4], grads[5], grads[6], grads[7], grads[8], grads[9], grads[10], grads[11], grads[12], grads[13], grads[14])
```

```python
import math

import jax
import jax.numpy as jnp
from jax import lax
from jax.sharding import Mesh
from jax.sharding import PartitionSpec as P

HEADS = 16
NOPE = 128
ROPE_D = 64
VD = 128
KVR = 512
TOP = 6
P_DEV = 64
C_DEV = 64
EPS = 1e-06

CTX = "context"
EXP = ("chip", "core")
ALL = ("context", "chip", "core")
BF = jnp.bfloat16
F32 = jnp.float32


def mm(left, right):
    return lax.dot_general(left, right, (((1,), (0,)), ((), ())), preferred_element_type=F32)


def mm_tn(left, right):
    return lax.dot_general(left, right, (((0,), (0,)), ((), ())), preferred_element_type=F32)


def mm_nt(left, right):
    return lax.dot_general(left, right, (((1,), (1,)), ((), ())), preferred_element_type=F32)


def rotation(position, width):
    half = width // 2
    freqs = 10000.0 ** (-2.0 * jnp.arange(half).astype(F32) / width)
    angle = position.astype(F32)[:, None] * freqs[None, :]
    return (jnp.cos(angle), jnp.sin(angle))


def place_of(device, offset, prompt_total):
    return jnp.where(
        offset < P_DEV, device * P_DEV + offset, prompt_total + device * C_DEV + offset - P_DEV
    )


def norm_back(grad_out, normal, inv_root, gain):
    scaled = grad_out * gain
    grad_gain = jnp.sum(grad_out * normal, 0)
    grad_in = inv_root * (scaled - normal * jnp.mean(scaled * normal, -1, keepdims=True))
    return (grad_in, grad_gain)


def pad_columns(values, width):
    return jnp.pad(values, ((0, 0), (0, width - values.shape[1])))


def up_to(value, step):
    return -(-value // step) * step


def gather_ctx(values):
    return lax.all_gather(values, CTX, axis=0, tiled=True)


def scatter_ctx(values):
    return lax.psum_scatter(values, CTX, scatter_dimension=0, tiled=True)


def gather_all(values):
    return lax.all_gather(values, ALL, axis=0, tiled=True)


def scatter_all(values):
    return lax.psum_scatter(values, ALL, scatter_dimension=0, tiled=True)


def split_query(weight, parts):
    rows = weight.shape[0]
    heads = weight.reshape(rows, parts, HEADS // parts, NOPE + ROPE_D)
    half = NOPE + ROPE_D // 2
    return jnp.concatenate(
        [
            heads[..., :NOPE].reshape(rows, parts, -1),
            heads[..., NOPE:half].reshape(rows, parts, -1),
            heads[..., half:].reshape(rows, parts, -1),
        ],
        -1,
    )


def join_query(values, parts):
    rows = values.shape[0]
    own = HEADS // parts
    wide = own * NOPE
    narrow = own * (ROPE_D // 2)
    return jnp.concatenate(
        [
            values[..., :wide].reshape(rows, parts, own, NOPE),
            values[..., wide : wide + narrow].reshape(rows, parts, own, ROPE_D // 2),
            values[..., wide + narrow :].reshape(rows, parts, own, ROPE_D // 2),
        ],
        -1,
    ).reshape(rows, -1)


def split_up(weight, parts):
    rows = weight.shape[0]
    heads = weight.reshape(rows, parts, HEADS // parts, NOPE + VD)
    return jnp.concatenate(
        [heads[..., :NOPE].reshape(rows, parts, -1), heads[..., NOPE:].reshape(rows, parts, -1)], -1
    )


def join_up(values, parts):
    rows = values.shape[0]
    own = HEADS // parts
    return jnp.concatenate(
        [
            values[..., : own * NOPE].reshape(rows, parts, own, NOPE),
            values[..., own * NOPE :].reshape(rows, parts, own, VD),
        ],
        -1,
    ).reshape(rows, -1)


def to_heads(weight):
    swapped = lax.all_to_all(
        weight.transpose(1, 0, 2), CTX, split_axis=0, concat_axis=0, tiled=True
    )
    full = lax.all_gather(swapped, EXP, axis=1, tiled=True)
    return full.reshape(-1, full.shape[-1])


def from_heads(grad, parts):
    experts = lax.axis_size(EXP)
    width = grad.shape[-1]
    full = grad.astype(BF).reshape(parts, experts, -1, width).transpose(1, 0, 2, 3)
    own = lax.psum_scatter(full.reshape(-1, width), EXP, scatter_dimension=0, tiled=True)
    own = own.reshape(parts, -1, width)
    swapped = lax.all_to_all(own, CTX, split_axis=0, concat_axis=0, tiled=True)
    return swapped.transpose(1, 0, 2)


def shards(
    inputs,
    cotangent,
    expert_ids,
    attn_gain,
    query_weight,
    latent_down,
    latent_gain,
    latent_up,
    output_weight,
    ffn_gain,
    router_weight,
    shared_gate,
    shared_up,
    shared_down,
    expert_gate,
    expert_up,
    expert_down,
):
    parts = lax.axis_size(CTX)
    expert_devices = lax.axis_size(EXP)
    devices = parts * expert_devices
    my_part = lax.axis_index(CTX)
    my_expert = lax.axis_index(EXP)
    tok = inputs.shape[1]
    width = inputs.shape[2]
    group = tok * parts
    total = tok * devices
    rows = query_weight.shape[0]
    lat_rows = latent_gain.shape[0]
    expert_count = router_weight.shape[1]
    own_heads = HEADS // parts
    half = ROPE_D // 2
    low_width = KVR + ROPE_D
    attn_scale = 1.0 / math.sqrt(NOPE + ROPE_D)

    chosen = expert_ids[0]
    mask_own = jnp.sum(
        (chosen[:, :, None] == jnp.arange(expert_count)[None, None, :]).astype(F32), 1
    )
    mask_cols = tok * expert_count // rows
    pack_used = low_width + expert_count + 3
    pack = jnp.concatenate(
        [
            latent_down,
            router_weight,
            attn_gain[:, None],
            ffn_gain[:, None],
            jnp.pad(latent_gain, (0, rows - lat_rows))[:, None],
            mask_own.astype(BF).reshape(rows, mask_cols),
        ],
        1,
    )
    pack_full = gather_all(pad_columns(pack, up_to(pack_used + mask_cols, 128)))
    group_in = gather_ctx(inputs[0])
    weight_down = pack_full[:, :low_width]
    weight_router = pack_full[:, low_width : low_width + expert_count]
    gain_attn = pack_full[:, low_width + expert_count].astype(F32)
    gain_ffn = pack_full[:, low_width + expert_count + 1].astype(F32)
    gain_latent = (
        pack_full[:, low_width + expert_count + 2]
        .reshape(devices, rows)[:, :lat_rows]
        .reshape(KVR)
        .astype(F32)
    )
    mask = pack_full[:, pack_used : pack_used + mask_cols].reshape(total, expert_count).astype(F32)

    weight_query = to_heads(split_query(query_weight, parts))
    weight_up = to_heads(split_up(latent_up, parts))
    weight_output = lax.all_gather(output_weight, EXP, axis=0, tiled=True)
    own_sgate, own_sup = (
        lax.all_to_all(shared_gate, ALL, split_axis=1, concat_axis=0, tiled=True),
        lax.all_to_all(shared_up, ALL, split_axis=1, concat_axis=0, tiled=True),
    )
    chunks = max(1, total // 4096)
    all_cots = [
        gather_all(cotangent[0, i * tok // chunks : (i + 1) * tok // chunks]) for i in range(chunks)
    ]

    group_rows = jnp.arange(group)
    place = place_of(group_rows // tok, group_rows % tok, P_DEV * parts)
    allowed = place[None, :] <= place[:, None]
    cosine, sine = rotation(place, ROPE_D)
    cos_heads = jnp.tile(cosine, (1, own_heads))
    sin_heads = jnp.tile(sine, (1, own_heads))
    group_tokens = group_in.astype(F32)
    inv_root = lax.rsqrt(jnp.mean(group_tokens * group_tokens, -1, keepdims=True) + EPS)
    normed = (group_tokens * inv_root * gain_attn).astype(BF)
    query_raw = mm(normed, weight_query)
    wide = own_heads * NOPE
    narrow = own_heads * half
    query_nope = query_raw[:, :wide].astype(BF)
    query_first = query_raw[:, wide : wide + narrow]
    query_second = query_raw[:, wide + narrow :]
    turned_first = (query_first * cos_heads - query_second * sin_heads).astype(BF)
    turned_second = (query_first * sin_heads + query_second * cos_heads).astype(BF)
    query_rot = jnp.stack(
        [
            jnp.concatenate(
                [
                    query_nope[:, h * NOPE : (h + 1) * NOPE],
                    turned_first[:, h * half : (h + 1) * half],
                    turned_second[:, h * half : (h + 1) * half],
                ],
                1,
            )
            for h in range(own_heads)
        ]
    )
    latent_raw = mm(normed, weight_down)
    compressed = latent_raw[:, :KVR]
    latent_root = lax.rsqrt(jnp.mean(compressed * compressed, -1, keepdims=True) + EPS)
    latent_hat = compressed * latent_root
    latent_norm = (latent_hat * gain_latent).astype(BF)
    rope_first = latent_raw[:, KVR : KVR + half]
    rope_second = latent_raw[:, KVR + half :]
    key_rope = jnp.concatenate(
        [rope_first * cosine - rope_second * sine, rope_first * sine + rope_second * cosine], 1
    ).astype(BF)
    key_value = mm(latent_norm, weight_up).astype(BF)
    keys = jnp.stack(
        [
            jnp.concatenate([key_value[:, h * NOPE : (h + 1) * NOPE], key_rope], 1)
            for h in range(own_heads)
        ]
    )
    values = jnp.stack(
        [key_value[:, wide + h * VD : wide + (h + 1) * VD] for h in range(own_heads)]
    )
    scores = jnp.einsum("htd,hsd->hts", query_rot, keys, preferred_element_type=F32) * attn_scale
    scores = jnp.where(allowed[None], scores, -1e30)
    exp_scores = jnp.exp(scores - jnp.max(scores, -1, keepdims=True))
    probs = exp_scores / jnp.sum(exp_scores, -1, keepdims=True)
    weights_low = probs.astype(BF)
    attended = (
        jnp.einsum("hts,hsd->thd", weights_low, values, preferred_element_type=F32)
        .astype(BF)
        .reshape(group, own_heads * VD)
    )
    projected = scatter_ctx(mm(attended, weight_output).astype(BF)).astype(F32)
    tokens = inputs[0].astype(F32)
    hidden = tokens + projected
    inv_mid = lax.rsqrt(jnp.mean(hidden * hidden, -1, keepdims=True) + EPS)
    hidden_hat = hidden * inv_mid
    mixed = (hidden_hat * gain_ffn).astype(BF)

    exp_local, _, ff_own = expert_gate.shape
    routed = exp_local * ff_own
    own_units = routed + own_sgate.shape[1]
    weight_in = jnp.concatenate(
        [expert_gate[i] for i in range(exp_local)]
        + [own_sgate]
        + [expert_up[i] for i in range(exp_local)]
        + [own_sup, weight_router],
        1,
    )
    weight_out = jnp.concatenate([expert_down.reshape(routed, width), shared_down], 0)
    first_expert = my_expert * exp_local

    def run_units(all_mixed, all_cot, mask):
        count = all_mixed.shape[0]
        activations = mm(all_mixed, weight_in)
        gate_activation = activations[:, :own_units]
        up_activation = activations[:, own_units : 2 * own_units]
        probs_all = jax.nn.softmax(activations[:, 2 * own_units :], axis=-1)
        gates_local = lax.dynamic_slice(probs_all * mask, (0, first_expert), (count, exp_local))
        mask_local = lax.dynamic_slice(mask, (0, first_expert), (count, exp_local))
        gate_columns = jnp.concatenate(
            [jnp.broadcast_to(gates_local[:, i : i + 1], (count, ff_own)) for i in range(exp_local)]
            + [jnp.ones((count, own_units - routed), F32)],
            1,
        )
        sigma = jax.nn.sigmoid(gate_activation)
        gated = gate_activation * sigma
        unit = (gated * up_activation).astype(BF).astype(F32)
        scaled_unit = (unit * gate_columns).astype(BF)
        out_part = mm(scaled_unit, weight_out).astype(BF)
        grad_unit_raw = mm_nt(all_cot, weight_out)
        grad_gate_terms = grad_unit_raw * unit
        grad_gates = (
            jnp.concatenate(
                [
                    jnp.sum(grad_gate_terms[:, i * ff_own : (i + 1) * ff_own], 1, keepdims=True)
                    for i in range(exp_local)
                ],
                1,
            )
            * mask_local
        )
        grad_probs_part = lax.dynamic_update_slice(
            jnp.zeros((count, up_to(expert_count, 128)), F32), grad_gates, (0, first_expert)
        ).astype(BF)
        grad_unit = grad_unit_raw * gate_columns
        grad_gate_act = (
            grad_unit * up_activation * sigma * (1.0 + gate_activation * (1.0 - sigma))
        ).astype(BF)
        grad_up_act = (grad_unit * gated).astype(BF)
        grad_acts = jnp.concatenate([grad_gate_act, grad_up_act], 1)
        grad_mixed_part = mm_nt(grad_acts, weight_in[:, : 2 * own_units]).astype(BF)
        back = scatter_all(jnp.concatenate([grad_mixed_part, grad_probs_part], 1))
        out_sum = scatter_all(out_part)
        weight_grads = (
            tuple(
                mm_tn(all_mixed, grad[:, i * ff_own : (i + 1) * ff_own])
                for grad in (grad_gate_act, grad_up_act)
                for i in range(exp_local)
            ),
            mm_tn(all_mixed, grad_gate_act[:, routed:]),
            mm_tn(all_mixed, grad_up_act[:, routed:]),
            mm_tn(scaled_unit, all_cot),
        )
        return out_sum, back, weight_grads

    mask_tokens = mask.reshape(devices, tok, expert_count)
    runs = []
    for i in range(chunks):
        span = slice(i * tok // chunks, (i + 1) * tok // chunks)
        runs.append(
            run_units(
                gather_all(mixed[span]), all_cots[i], mask_tokens[:, span].reshape(-1, expert_count)
            )
        )
    out_sum = jnp.concatenate([r[0] for r in runs], 0).astype(F32)
    back = jnp.concatenate([r[1] for r in runs], 0).astype(F32)
    pair_grads, grad_sgate, grad_sup, grad_down_all = jax.tree.map(
        lambda *terms: sum(terms[1:], terms[0]), *[r[2] for r in runs]
    )
    output = hidden + out_sum
    expert_gate_total = jnp.stack(pair_grads[:exp_local])
    expert_up_total = jnp.stack(pair_grads[exp_local:])
    expert_down_total = grad_down_all[:routed].reshape(exp_local, ff_own, width)
    sum_sdown = grad_down_all[routed:]
    sum_sgate, sum_sup = (
        lax.all_to_all(
            grad_sgate.astype(BF), ALL, split_axis=0, concat_axis=1, tiled=True
        ).astype(F32),
        lax.all_to_all(grad_sup.astype(BF), ALL, split_axis=0, concat_axis=1, tiled=True).astype(
            F32
        ),
    )

    grad_probs = back[:, width : width + expert_count]
    router_probs = jax.nn.softmax(mm(mixed, weight_router), axis=-1)
    grad_logits = (
        router_probs * (grad_probs - jnp.sum(router_probs * grad_probs, -1, keepdims=True))
    ).astype(BF)
    grad_router = mm_tn(mixed, grad_logits)
    grad_mixed = back[:, :width] + mm_nt(grad_logits, weight_router)
    grad_mid, grad_gain_ffn = norm_back(grad_mixed, hidden_hat, inv_mid, gain_ffn)
    grad_hidden = cotangent[0].astype(F32) + grad_mid
    grad_proj = gather_ctx(grad_hidden.astype(BF))
    sum_output = lax.psum_scatter(
        mm_tn(attended, grad_proj).astype(BF), EXP, scatter_dimension=0, tiled=True
    ).astype(F32)
    grad_att = mm_nt(grad_proj, weight_output).astype(BF)
    grad_att = jnp.stack([grad_att[:, h * VD : (h + 1) * VD] for h in range(own_heads)])
    grad_weights = jnp.einsum("htd,hsd->hts", grad_att, values, preferred_element_type=F32)
    grad_values = jnp.einsum("hts,htd->shd", weights_low, grad_att, preferred_element_type=F32)
    grad_scores = (
        probs * (grad_weights - jnp.sum(probs * grad_weights, -1, keepdims=True))
    ).astype(BF)
    grad_query = (
        jnp.einsum("hts,hsd->htd", grad_scores, keys, preferred_element_type=F32) * attn_scale
    )
    grad_keys = (
        jnp.einsum("hts,htd->hsd", grad_scores, query_rot, preferred_element_type=F32) * attn_scale
    )
    grad_first = jnp.concatenate(
        [grad_query[h, :, NOPE : NOPE + half] for h in range(own_heads)], 1
    )
    grad_second = jnp.concatenate([grad_query[h, :, NOPE + half :] for h in range(own_heads)], 1)
    grad_qraw = jnp.concatenate(
        [grad_query[h, :, :NOPE] for h in range(own_heads)]
        + [
            grad_first * cos_heads + grad_second * sin_heads,
            grad_second * cos_heads - grad_first * sin_heads,
        ],
        1,
    ).astype(BF)
    grad_kv = jnp.concatenate(
        [grad_keys[h, :, :NOPE] for h in range(own_heads)]
        + [grad_values.reshape(group, own_heads * VD)],
        1,
    ).astype(BF)
    grad_low = jnp.concatenate(
        [mm_nt(grad_kv, weight_up), jnp.sum(grad_keys[:, :, NOPE:], 0)], 1
    )
    grad_low = scatter_ctx(pad_columns(grad_low.astype(BF), up_to(low_width, 128))).astype(F32)
    grad_front = scatter_ctx(mm_nt(grad_qraw, weight_query).astype(BF)).astype(F32)
    sum_query = join_query(from_heads(mm_tn(normed, grad_qraw), parts), parts).astype(F32)
    sum_up = join_up(from_heads(mm_tn(latent_norm, grad_kv), parts), parts).astype(F32)

    def own(values):
        return lax.dynamic_slice_in_dim(values, my_part * tok, tok, 0)

    cos_own, sin_own = own(cosine), own(sine)
    grad_comp, grad_gain_latent = norm_back(
        grad_low[:, :KVR], own(latent_hat), own(latent_root), gain_latent
    )
    rope_grad_first = grad_low[:, KVR : KVR + half]
    rope_grad_second = grad_low[:, KVR + half : low_width]
    grad_lraw = jnp.concatenate(
        [
            grad_comp,
            rope_grad_first * cos_own + rope_grad_second * sin_own,
            rope_grad_second * cos_own - rope_grad_first * sin_own,
        ],
        1,
    ).astype(BF)
    normed_own = own(normed)
    grad_down = mm_tn(normed_own, grad_lraw)
    grad_normed = grad_front + mm_nt(grad_lraw, weight_down)
    inv_own = own(inv_root)
    grad_entry, grad_gain_attn = norm_back(grad_normed, tokens * inv_own, inv_own, gain_attn)
    grad_inputs = grad_hidden + grad_entry

    pack_grad = jnp.concatenate(
        [
            grad_down,
            grad_router,
            grad_gain_attn[:, None],
            grad_gain_ffn[:, None],
            jnp.pad(
                grad_gain_latent.reshape(devices, lat_rows), ((0, 0), (0, rows - lat_rows))
            ).reshape(width, 1),
        ],
        1,
    ).astype(BF)
    pack_sum = scatter_all(pad_columns(pack_grad, up_to(pack_used, 128))).astype(F32)
    return (
        output.astype(BF)[None],
        grad_inputs[None],
        pack_sum[:, low_width + expert_count],
        sum_query,
        pack_sum[:, :low_width],
        pack_sum[:lat_rows, low_width + expert_count + 2],
        sum_up,
        sum_output,
        pack_sum[:, low_width + expert_count + 1],
        pack_sum[:, low_width : low_width + expert_count],
        sum_sgate,
        sum_sup,
        sum_sdown,
        expert_gate_total,
        expert_up_total,
        expert_down_total,
    )


def solution(mesh):
    context, experts = mesh.devices.shape
    split = Mesh(mesh.devices.reshape(context, experts // 2, 2), ALL)
    tokens = P(EXP, CTX, None)
    dense = P(ALL, None)
    gain = P(ALL)
    columns = P(EXP, None, CTX)
    down = P(EXP, CTX, None)
    in_specs = (
        tokens, tokens, tokens, gain, dense, dense, gain, dense, dense, gain, dense, dense, dense,
        dense, columns, columns, down,
    )
    out_specs = (
        tokens, tokens, gain, dense, dense, gain, dense, dense, gain, dense, dense, dense, dense,
        columns, columns, down,
    )
    return jax.shard_map(shards, mesh=split, in_specs=in_specs, out_specs=out_specs, check_vma=False)
```

```python
import math

import jax
import jax.numpy as jnp
from jax import lax
from jax.sharding import Mesh
from jax.sharding import PartitionSpec as P

HEADS = 16
NOPE = 128
ROPE_D = 64
VD = 128
KVR = 512
TOP = 6
P_DEV = 64
C_DEV = 64
EPS = 1e-06

CTX = "context"
EXP = ("chip", "core")
ALL = ("context", "chip", "core")
BF = jnp.bfloat16
F32 = jnp.float32


def mm(left, right):
    return lax.dot_general(left, right, (((1,), (0,)), ((), ())), preferred_element_type=F32)


def mm_tn(left, right):
    return lax.dot_general(left, right, (((0,), (0,)), ((), ())), preferred_element_type=F32)


def mm_nt(left, right):
    return lax.dot_general(left, right, (((1,), (1,)), ((), ())), preferred_element_type=F32)


def rotation(position, width):
    half = width // 2
    freqs = 10000.0 ** (-2.0 * jnp.arange(half).astype(F32) / width)
    angle = position.astype(F32)[:, None] * freqs[None, :]
    return (jnp.cos(angle), jnp.sin(angle))


def place_of(device, offset, prompt_total):
    return jnp.where(
        offset < P_DEV, device * P_DEV + offset, prompt_total + device * C_DEV + offset - P_DEV
    )


def norm_back(grad_out, normal, inv_root, gain):
    scaled = grad_out * gain
    grad_gain = jnp.sum(grad_out * normal, 0)
    grad_in = inv_root * (scaled - normal * jnp.mean(scaled * normal, -1, keepdims=True))
    return (grad_in, grad_gain)


def pad_columns(values, width):
    return jnp.pad(values, ((0, 0), (0, width - values.shape[1])))


def up_to(value, step):
    return -(-value // step) * step


def hop(values, flip):
    return lax.ppermute(values, CTX, [(i, i ^ flip) for i in range(4)])


def by_part(pieces):
    own = lax.axis_index(CTX)
    low = (own & 1) == 1
    high = (own & 2) == 2
    first = [jnp.where(low, pieces[a ^ 1], pieces[a]) for a in range(4)]
    return [jnp.where(high, first[a ^ 2], first[a]) for a in range(4)]


def gather_ctx(values):
    half = values.shape[0] // 2
    one = hop(values, 1)
    two = hop(values, 2)
    return jnp.concatenate([values, one, two, hop(two[:half], 1), hop(one[half:], 2)], 0)


def scatter_ctx(values):
    tok = values.shape[0] // 4
    half = tok // 2
    head = [values[j * tok : j * tok + half] for j in range(4)]
    tail = [values[j * tok + half : (j + 1) * tok] for j in range(4)]
    head_pass = hop(head[3], 1)
    tail_pass = hop(tail[3], 2)
    head_own = hop(head[1], 1)
    tail_own = hop(tail[2], 2)
    head_last = hop((head[2].astype(F32) + head_pass.astype(F32)).astype(BF), 2)
    tail_last = hop((tail[1].astype(F32) + tail_pass.astype(F32)).astype(BF), 1)
    return jnp.concatenate(
        [
            head[0].astype(F32) + head_own.astype(F32) + head_last.astype(F32),
            tail[0].astype(F32) + tail_own.astype(F32) + tail_last.astype(F32),
        ],
        0,
    )


def gather_all(values):
    return lax.all_gather(values, ALL, axis=0, tiled=True)


def scatter_all(values):
    return lax.psum_scatter(values, ALL, scatter_dimension=0, tiled=True)


def split_query(weight, parts):
    rows = weight.shape[0]
    heads = weight.reshape(rows, parts, HEADS // parts, NOPE + ROPE_D)
    half = NOPE + ROPE_D // 2
    return jnp.concatenate(
        [
            heads[..., :NOPE].reshape(rows, parts, -1),
            heads[..., NOPE:half].reshape(rows, parts, -1),
            heads[..., half:].reshape(rows, parts, -1),
        ],
        -1,
    )


def join_query(values, parts):
    rows = values.shape[0]
    own = HEADS // parts
    wide = own * NOPE
    narrow = own * (ROPE_D // 2)
    return jnp.concatenate(
        [
            values[..., :wide].reshape(rows, parts, own, NOPE),
            values[..., wide : wide + narrow].reshape(rows, parts, own, ROPE_D // 2),
            values[..., wide + narrow :].reshape(rows, parts, own, ROPE_D // 2),
        ],
        -1,
    ).reshape(rows, -1)


def split_up(weight, parts):
    rows = weight.shape[0]
    heads = weight.reshape(rows, parts, HEADS // parts, NOPE + VD)
    return jnp.concatenate(
        [heads[..., :NOPE].reshape(rows, parts, -1), heads[..., NOPE:].reshape(rows, parts, -1)], -1
    )


def join_up(values, parts):
    rows = values.shape[0]
    own = HEADS // parts
    return jnp.concatenate(
        [
            values[..., : own * NOPE].reshape(rows, parts, own, NOPE),
            values[..., own * NOPE :].reshape(rows, parts, own, VD),
        ],
        -1,
    ).reshape(rows, -1)


def swap_parts(pieces):
    ordered = by_part(pieces)
    return by_part([ordered[0]] + [hop(ordered[j], j) for j in range(1, 4)])


def gather_exp(pieces):
    full = lax.all_gather(jnp.stack(pieces), EXP, axis=1, tiled=True)
    return full.reshape(-1, full.shape[-1])


def to_heads(weight):
    return gather_exp(swap_parts([weight[:, j] for j in range(4)]))


def from_heads(grad, parts):
    experts = lax.axis_size(EXP)
    width = grad.shape[-1]
    full = grad.astype(BF).reshape(parts, experts, -1, width).transpose(1, 0, 2, 3)
    own = lax.psum_scatter(full.reshape(-1, width), EXP, scatter_dimension=0, tiled=True)
    own = own.reshape(parts, -1, width)
    return jnp.stack(swap_parts([own[a] for a in range(4)]), 1)


def shards(
    inputs,
    cotangent,
    expert_ids,
    attn_gain,
    query_weight,
    latent_down,
    latent_gain,
    latent_up,
    output_weight,
    ffn_gain,
    router_weight,
    shared_gate,
    shared_up,
    shared_down,
    expert_gate,
    expert_up,
    expert_down,
):
    parts = lax.axis_size(CTX)
    expert_devices = lax.axis_size(EXP)
    devices = parts * expert_devices
    my_part = lax.axis_index(CTX)
    my_expert = lax.axis_index(EXP)
    tok = inputs.shape[1]
    width = inputs.shape[2]
    group = tok * parts
    total = tok * devices
    rows = query_weight.shape[0]
    lat_rows = latent_gain.shape[0]
    expert_count = router_weight.shape[1]
    own_heads = HEADS // parts
    half = ROPE_D // 2
    low_width = KVR + ROPE_D
    attn_scale = 1.0 / math.sqrt(NOPE + ROPE_D)

    chosen = expert_ids[0]
    mask_own = jnp.sum(
        (chosen[:, :, None] == jnp.arange(expert_count)[None, None, :]).astype(F32), 1
    )
    mask_cols = tok * expert_count // rows
    pack_used = low_width + expert_count + 3
    pack = jnp.concatenate(
        [
            latent_down,
            router_weight,
            attn_gain[:, None],
            ffn_gain[:, None],
            jnp.pad(latent_gain, (0, rows - lat_rows))[:, None],
            mask_own.astype(BF).reshape(rows, mask_cols),
        ],
        1,
    )
    pack = pad_columns(pack, up_to(pack_used + mask_cols, 128))
    pack_full = gather_exp(by_part([pack] + [hop(pack, j) for j in range(1, 4)]))
    group_in = gather_ctx(inputs[0])
    weight_down = pack_full[:, :low_width]
    weight_router = pack_full[:, low_width : low_width + expert_count]
    gain_attn = pack_full[:, low_width + expert_count].astype(F32)
    gain_ffn = pack_full[:, low_width + expert_count + 1].astype(F32)
    gain_latent = (
        pack_full[:, low_width + expert_count + 2]
        .reshape(devices, rows)[:, :lat_rows]
        .reshape(KVR)
        .astype(F32)
    )
    mask = pack_full[:, pack_used : pack_used + mask_cols].reshape(total, expert_count).astype(F32)

    weight_query = to_heads(split_query(query_weight, parts))
    weight_up = to_heads(split_up(latent_up, parts))
    weight_output = lax.all_gather(output_weight, EXP, axis=0, tiled=True)
    own_sgate, own_sup = (
        lax.all_to_all(shared_gate, ALL, split_axis=1, concat_axis=0, tiled=True),
        lax.all_to_all(shared_up, ALL, split_axis=1, concat_axis=0, tiled=True),
    )
    chunks = max(1, total // 4096)

    group_rows = jnp.arange(group)
    place = place_of(my_part ^ (group_rows // tok), group_rows % tok, P_DEV * parts)
    allowed = place[None, :] <= place[:, None]
    cosine, sine = rotation(place, ROPE_D)
    cos_heads = jnp.tile(cosine, (1, own_heads))
    sin_heads = jnp.tile(sine, (1, own_heads))
    group_tokens = group_in.astype(F32)
    inv_root = lax.rsqrt(jnp.mean(group_tokens * group_tokens, -1, keepdims=True) + EPS)
    normed = (group_tokens * inv_root * gain_attn).astype(BF)
    query_raw = mm(normed, weight_query)
    wide = own_heads * NOPE
    narrow = own_heads * half
    query_nope = query_raw[:, :wide].astype(BF)
    query_first = query_raw[:, wide : wide + narrow]
    query_second = query_raw[:, wide + narrow :]
    turned_first = (query_first * cos_heads - query_second * sin_heads).astype(BF)
    turned_second = (query_first * sin_heads + query_second * cos_heads).astype(BF)
    query_rot = jnp.stack(
        [
            jnp.concatenate(
                [
                    query_nope[:, h * NOPE : (h + 1) * NOPE],
                    turned_first[:, h * half : (h + 1) * half],
                    turned_second[:, h * half : (h + 1) * half],
                ],
                1,
            )
            for h in range(own_heads)
        ]
    )
    latent_raw = mm(normed, weight_down)
    compressed = latent_raw[:, :KVR]
    latent_root = lax.rsqrt(jnp.mean(compressed * compressed, -1, keepdims=True) + EPS)
    latent_hat = compressed * latent_root
    latent_norm = (latent_hat * gain_latent).astype(BF)
    rope_first = latent_raw[:, KVR : KVR + half]
    rope_second = latent_raw[:, KVR + half :]
    key_rope = jnp.concatenate(
        [rope_first * cosine - rope_second * sine, rope_first * sine + rope_second * cosine], 1
    ).astype(BF)
    key_value = mm(latent_norm, weight_up).astype(BF)
    keys = jnp.stack(
        [
            jnp.concatenate([key_value[:, h * NOPE : (h + 1) * NOPE], key_rope], 1)
            for h in range(own_heads)
        ]
    )
    values = jnp.stack(
        [key_value[:, wide + h * VD : wide + (h + 1) * VD] for h in range(own_heads)]
    )
    scores = jnp.einsum("htd,hsd->hts", query_rot, keys, preferred_element_type=F32) * attn_scale
    scores = jnp.where(allowed[None], scores, -1e30)
    exp_scores = jnp.exp(scores - jnp.max(scores, -1, keepdims=True))
    probs = exp_scores / jnp.sum(exp_scores, -1, keepdims=True)
    weights_low = probs.astype(BF)
    attended = (
        jnp.einsum("hts,hsd->thd", weights_low, values, preferred_element_type=F32)
        .astype(BF)
        .reshape(group, own_heads * VD)
    )
    projected = scatter_ctx(mm(attended, weight_output).astype(BF))
    tokens = inputs[0].astype(F32)
    hidden = tokens + projected
    inv_mid = lax.rsqrt(jnp.mean(hidden * hidden, -1, keepdims=True) + EPS)
    hidden_hat = hidden * inv_mid
    mixed = (hidden_hat * gain_ffn).astype(BF)

    exp_local, _, ff_own = expert_gate.shape
    routed = exp_local * ff_own
    own_units = routed + own_sgate.shape[1]
    weight_in = jnp.concatenate(
        [expert_gate[i] for i in range(exp_local)]
        + [own_sgate]
        + [expert_up[i] for i in range(exp_local)]
        + [own_sup, weight_router],
        1,
    )
    weight_out = jnp.concatenate([expert_down.reshape(routed, width), shared_down], 0)
    first_expert = my_expert * exp_local

    def run_units(all_mixed, all_cot, mask):
        count = all_mixed.shape[0]
        activations = mm(all_mixed, weight_in)
        gate_activation = activations[:, :own_units]
        up_activation = activations[:, own_units : 2 * own_units]
        probs_all = jax.nn.softmax(activations[:, 2 * own_units :], axis=-1)
        gates_local = lax.dynamic_slice(probs_all * mask, (0, first_expert), (count, exp_local))
        mask_local = lax.dynamic_slice(mask, (0, first_expert), (count, exp_local))
        gate_columns = jnp.concatenate(
            [jnp.broadcast_to(gates_local[:, i : i + 1], (count, ff_own)) for i in range(exp_local)]
            + [jnp.ones((count, own_units - routed), F32)],
            1,
        )
        sigma = jax.nn.sigmoid(gate_activation)
        gated = gate_activation * sigma
        unit = (gated * up_activation).astype(BF).astype(F32)
        scaled_unit = (unit * gate_columns).astype(BF)
        out_part = mm(scaled_unit, weight_out).astype(BF)
        grad_unit_raw = mm_nt(all_cot, weight_out)
        grad_gate_terms = grad_unit_raw * unit
        grad_gates = (
            jnp.concatenate(
                [
                    jnp.sum(grad_gate_terms[:, i * ff_own : (i + 1) * ff_own], 1, keepdims=True)
                    for i in range(exp_local)
                ],
                1,
            )
            * mask_local
        )
        grad_probs_part = lax.dynamic_update_slice(
            jnp.zeros((count, up_to(expert_count, 128)), F32), grad_gates, (0, first_expert)
        ).astype(BF)
        grad_unit = grad_unit_raw * gate_columns
        grad_gate_act = (
            grad_unit * up_activation * sigma * (1.0 + gate_activation * (1.0 - sigma))
        ).astype(BF)
        grad_up_act = (grad_unit * gated).astype(BF)
        grad_acts = jnp.concatenate([grad_gate_act, grad_up_act], 1)
        grad_mixed_part = mm_nt(grad_acts, weight_in[:, : 2 * own_units]).astype(BF)
        back = scatter_all(jnp.concatenate([grad_mixed_part, grad_probs_part], 1))
        out_sum = scatter_all(out_part)
        weight_grads = (
            tuple(
                mm_tn(all_mixed, grad[:, i * ff_own : (i + 1) * ff_own])
                for grad in (grad_gate_act, grad_up_act)
                for i in range(exp_local)
            ),
            mm_tn(all_mixed, grad_gate_act[:, routed:]),
            mm_tn(all_mixed, grad_up_act[:, routed:]),
            mm_tn(scaled_unit, all_cot),
        )
        return out_sum, back, weight_grads

    mask_tokens = mask.reshape(devices, tok, expert_count)
    runs = []
    for i in range(chunks):
        span = slice(i * tok // chunks, (i + 1) * tok // chunks)
        own_mixed, own_cot = mixed[span], cotangent[0, span]
        if runs:
            own_mixed, own_cot, _ = lax.optimization_barrier((own_mixed, own_cot, runs[-1][:2]))
        runs.append(
            run_units(
                gather_all(own_mixed),
                gather_all(own_cot),
                mask_tokens[:, span].reshape(-1, expert_count),
            )
        )
    out_sum = jnp.concatenate([r[0] for r in runs], 0).astype(F32)
    back = jnp.concatenate([r[1] for r in runs], 0).astype(F32)
    pair_grads, grad_sgate, grad_sup, grad_down_all = jax.tree.map(
        lambda *terms: sum(terms[1:], terms[0]), *[r[2] for r in runs]
    )
    output = hidden + out_sum
    expert_gate_total = jnp.stack(pair_grads[:exp_local])
    expert_up_total = jnp.stack(pair_grads[exp_local:])
    expert_down_total = grad_down_all[:routed].reshape(exp_local, ff_own, width)
    sum_sdown = grad_down_all[routed:]
    sum_sgate, sum_sup = (
        lax.all_to_all(
            grad_sgate.astype(BF), ALL, split_axis=0, concat_axis=1, tiled=True
        ).astype(F32),
        lax.all_to_all(grad_sup.astype(BF), ALL, split_axis=0, concat_axis=1, tiled=True).astype(
            F32
        ),
    )

    grad_probs = back[:, width : width + expert_count]
    router_probs = jax.nn.softmax(mm(mixed, weight_router), axis=-1)
    grad_logits = (
        router_probs * (grad_probs - jnp.sum(router_probs * grad_probs, -1, keepdims=True))
    ).astype(BF)
    grad_router = mm_tn(mixed, grad_logits)
    grad_mixed = back[:, :width] + mm_nt(grad_logits, weight_router)
    grad_mid, grad_gain_ffn = norm_back(grad_mixed, hidden_hat, inv_mid, gain_ffn)
    grad_hidden = cotangent[0].astype(F32) + grad_mid
    grad_proj = gather_ctx(grad_hidden.astype(BF))
    sum_output = lax.psum_scatter(
        mm_tn(attended, grad_proj).astype(BF), EXP, scatter_dimension=0, tiled=True
    ).astype(F32)
    grad_att = mm_nt(grad_proj, weight_output).astype(BF)
    grad_att = jnp.stack([grad_att[:, h * VD : (h + 1) * VD] for h in range(own_heads)])
    grad_weights = jnp.einsum("htd,hsd->hts", grad_att, values, preferred_element_type=F32)
    grad_values = jnp.einsum("hts,htd->shd", weights_low, grad_att, preferred_element_type=F32)
    grad_scores = (
        probs * (grad_weights - jnp.sum(probs * grad_weights, -1, keepdims=True))
    ).astype(BF)
    grad_query = (
        jnp.einsum("hts,hsd->htd", grad_scores, keys, preferred_element_type=F32) * attn_scale
    )
    grad_keys = (
        jnp.einsum("hts,htd->hsd", grad_scores, query_rot, preferred_element_type=F32) * attn_scale
    )
    grad_first = jnp.concatenate(
        [grad_query[h, :, NOPE : NOPE + half] for h in range(own_heads)], 1
    )
    grad_second = jnp.concatenate([grad_query[h, :, NOPE + half :] for h in range(own_heads)], 1)
    grad_qraw = jnp.concatenate(
        [grad_query[h, :, :NOPE] for h in range(own_heads)]
        + [
            grad_first * cos_heads + grad_second * sin_heads,
            grad_second * cos_heads - grad_first * sin_heads,
        ],
        1,
    ).astype(BF)
    grad_kv = jnp.concatenate(
        [grad_keys[h, :, :NOPE] for h in range(own_heads)]
        + [grad_values.reshape(group, own_heads * VD)],
        1,
    ).astype(BF)
    grad_low = jnp.concatenate(
        [mm_nt(grad_kv, weight_up), jnp.sum(grad_keys[:, :, NOPE:], 0)], 1
    )
    grad_low = scatter_ctx(pad_columns(grad_low.astype(BF), up_to(low_width, 128)))
    grad_front = scatter_ctx(mm_nt(grad_qraw, weight_query).astype(BF))
    sum_query = join_query(from_heads(mm_tn(normed, grad_qraw), parts), parts).astype(F32)
    sum_up = join_up(from_heads(mm_tn(latent_norm, grad_kv), parts), parts).astype(F32)

    def own(values):
        return values[:tok]

    cos_own, sin_own = own(cosine), own(sine)
    grad_comp, grad_gain_latent = norm_back(
        grad_low[:, :KVR], own(latent_hat), own(latent_root), gain_latent
    )
    rope_grad_first = grad_low[:, KVR : KVR + half]
    rope_grad_second = grad_low[:, KVR + half : low_width]
    grad_lraw = jnp.concatenate(
        [
            grad_comp,
            rope_grad_first * cos_own + rope_grad_second * sin_own,
            rope_grad_second * cos_own - rope_grad_first * sin_own,
        ],
        1,
    ).astype(BF)
    normed_own = own(normed)
    grad_down = mm_tn(normed_own, grad_lraw)
    grad_normed = grad_front + mm_nt(grad_lraw, weight_down)
    inv_own = own(inv_root)
    grad_entry, grad_gain_attn = norm_back(grad_normed, tokens * inv_own, inv_own, gain_attn)
    grad_inputs = grad_hidden + grad_entry

    pack_grad = jnp.concatenate(
        [
            grad_down,
            grad_router,
            grad_gain_attn[:, None],
            grad_gain_ffn[:, None],
            jnp.pad(
                grad_gain_latent.reshape(devices, lat_rows), ((0, 0), (0, rows - lat_rows))
            ).reshape(width, 1),
        ],
        1,
    ).astype(BF)
    pack_grad = pad_columns(pack_grad, up_to(pack_used, 128)).reshape(parts, width // parts, -1)
    pack_half = scatter_ctx(jnp.concatenate(by_part([pack_grad[a] for a in range(parts)]), 0))
    pack_sum = lax.psum_scatter(
        pack_half.astype(BF), EXP, scatter_dimension=0, tiled=True
    ).astype(F32)
    return (
        output.astype(BF)[None],
        grad_inputs[None],
        pack_sum[:, low_width + expert_count],
        sum_query,
        pack_sum[:, :low_width],
        pack_sum[:lat_rows, low_width + expert_count + 2],
        sum_up,
        sum_output,
        pack_sum[:, low_width + expert_count + 1],
        pack_sum[:, low_width : low_width + expert_count],
        sum_sgate,
        sum_sup,
        sum_sdown,
        expert_gate_total,
        expert_up_total,
        expert_down_total,
    )


def solution(mesh):
    context, experts = mesh.devices.shape
    split = Mesh(mesh.devices.reshape(context, experts // 2, 2), ALL)
    tokens = P(EXP, CTX, None)
    dense = P(ALL, None)
    gain = P(ALL)
    columns = P(EXP, None, CTX)
    down = P(EXP, CTX, None)
    in_specs = (
        tokens, tokens, tokens, gain, dense, dense, gain, dense, dense, gain, dense, dense, dense,
        dense, columns, columns, down,
    )
    out_specs = (
        tokens, tokens, gain, dense, dense, gain, dense, dense, gain, dense, dense, dense, dense,
        columns, columns, down,
    )
    return jax.shard_map(shards, mesh=split, in_specs=in_specs, out_specs=out_specs, check_vma=False)
```

```python
import math

import jax
import jax.numpy as jnp
from jax import lax
from jax.sharding import Mesh
from jax.sharding import PartitionSpec as P

HEADS = 16
NOPE = 128
ROPE_D = 64
VD = 128
KVR = 512
TOP = 6
P_DEV = 64
C_DEV = 64
EPS = 1e-06

CTX = "context"
EXP = ("chip", "core")
ALL = ("context", "chip", "core")
BF = jnp.bfloat16
F32 = jnp.float32


def mm(left, right):
    return lax.dot_general(left, right, (((1,), (0,)), ((), ())), preferred_element_type=F32)


def mm_tn(left, right):
    return lax.dot_general(left, right, (((0,), (0,)), ((), ())), preferred_element_type=F32)


def mm_nt(left, right):
    return lax.dot_general(left, right, (((1,), (1,)), ((), ())), preferred_element_type=F32)


def rotation(position, width):
    half = width // 2
    freqs = 10000.0 ** (-2.0 * jnp.arange(half).astype(F32) / width)
    angle = position.astype(F32)[:, None] * freqs[None, :]
    return (jnp.cos(angle), jnp.sin(angle))


def place_of(device, offset, prompt_total):
    return jnp.where(
        offset < P_DEV, device * P_DEV + offset, prompt_total + device * C_DEV + offset - P_DEV
    )


def norm_back(grad_out, normal, inv_root, gain):
    scaled = grad_out * gain
    grad_gain = jnp.sum(grad_out * normal, 0)
    grad_in = inv_root * (scaled - normal * jnp.mean(scaled * normal, -1, keepdims=True))
    return (grad_in, grad_gain)


def pad_columns(values, width):
    return jnp.pad(values, ((0, 0), (0, width - values.shape[1])))


def up_to(value, step):
    return -(-value // step) * step


def hop(values, flip):
    return lax.ppermute(values, CTX, [(i, i ^ flip) for i in range(4)])


def by_part(pieces):
    own = lax.axis_index(CTX)
    low = (own & 1) == 1
    high = (own & 2) == 2
    first = [jnp.where(low, pieces[a ^ 1], pieces[a]) for a in range(4)]
    return [jnp.where(high, first[a ^ 2], first[a]) for a in range(4)]


def gather_ctx(values):
    half = values.shape[0] // 2
    one = hop(values, 1)
    two = hop(values, 2)
    return jnp.concatenate([values, one, two, hop(two[:half], 1), hop(one[half:], 2)], 0)


def scatter_ctx(values):
    tok = values.shape[0] // 4
    return scatter_pieces([values[j * tok : (j + 1) * tok] for j in range(4)])


def scatter_pieces(pieces):
    half = pieces[0].shape[0] // 2
    head = [piece[:half] for piece in pieces]
    tail = [piece[half:] for piece in pieces]
    head_pass = hop(head[3], 1)
    tail_pass = hop(tail[3], 2)
    head_own = hop(head[1], 1)
    tail_own = hop(tail[2], 2)
    head_last = hop((head[2].astype(F32) + head_pass.astype(F32)).astype(BF), 2)
    tail_last = hop((tail[1].astype(F32) + tail_pass.astype(F32)).astype(BF), 1)
    return jnp.concatenate(
        [
            head[0].astype(F32) + head_own.astype(F32) + head_last.astype(F32),
            tail[0].astype(F32) + tail_own.astype(F32) + tail_last.astype(F32),
        ],
        0,
    )


def gather_all(values):
    return lax.all_gather(values, ALL, axis=0, tiled=True)


def scatter_all(values):
    return lax.psum_scatter(values, ALL, scatter_dimension=0, tiled=True)


def swap_core(values):
    return lax.ppermute(values, "core", [(0, 1), (1, 0)])


def shift_chip(values, step):
    return lax.ppermute(values, "chip", [(i, (i + step) % 4) for i in range(4)])


def put(target, values, *place):
    return lax.dynamic_update_slice(target, values, place + (0,) * (target.ndim - len(place)))


def gather_line(values):
    chip = lax.axis_index("chip")
    line = jnp.zeros((4,) + values.shape, values.dtype)
    for step in range(4):
        piece = shift_chip(values, step) if step else values
        line = put(line, piece[None], (chip - step) % 4)
    return line


def gather_plane(line):
    one = hop(line, 1)
    two = hop(line, 2)
    return [line, one, two, hop(two[:2], 1), hop(one[2:], 2)]


def gather_cores(pieces):
    _, tok, width = pieces[0].shape
    part, _, core = (lax.axis_index(a) for a in ALL)
    full = jnp.zeros((4, 4, 2, tok, width), pieces[0].dtype)
    for piece, flip, first in zip(pieces, (0, 1, 2, 3, 3), (0, 0, 0, 0, 2)):
        other = swap_core(piece)
        full = put(full, piece[None, :, None], part ^ flip, first, core)
        full = put(full, other[None, :, None], part ^ flip, first, 1 - core)
    return full.reshape(-1, width)


def scatter_line(values, axis_values):
    chip = lax.axis_index("chip")
    total = lax.dynamic_index_in_dim(values, chip, 0, False)
    for step in range(1, 4):
        block = lax.dynamic_index_in_dim(axis_values, (chip + step) % 4, 0, False)
        total = total + shift_chip(block, step).astype(F32)
    return total


def add_cores(blocks):
    core = lax.axis_index("core")
    axis = blocks.ndim - 3
    away = swap_core(lax.dynamic_index_in_dim(blocks, 1 - core, axis, False))
    return lax.dynamic_index_in_dim(blocks, core, axis, False).astype(F32) + away.astype(F32)


def scatter_tokens(values, fills):
    if lax.axis_size("chip") != 4:
        return scatter_all(values).astype(F32), fills
    width = values.shape[1]
    blocks = values.reshape(4, 4, 2, -1, width)
    part = lax.axis_index(CTX)
    sums = [None] * 4
    for j in (3, 1, 2, 0):
        block = lax.dynamic_index_in_dim(blocks, part ^ j, 0, False)
        sums[j] = add_cores(block).astype(BF).reshape(-1, width)
    sums, first = lax.optimization_barrier((sums, fills[0]))
    own, second = lax.optimization_barrier((scatter_pieces(sums), fills[1]))
    own = own.reshape(4, -1, width)
    total, third = lax.optimization_barrier((scatter_line(own, own.astype(BF)), fills[2]))
    return total, (first, second, third)


def scatter_exp(values):
    if lax.axis_size("chip") != 4:
        return lax.psum_scatter(values, EXP, scatter_dimension=0, tiled=True).astype(F32)
    own = add_cores(values.reshape(4, 2, -1, values.shape[1]))
    return scatter_line(own, own.astype(BF))


def split_query(weight, parts):
    rows = weight.shape[0]
    heads = weight.reshape(rows, parts, HEADS // parts, NOPE + ROPE_D)
    half = NOPE + ROPE_D // 2
    return jnp.concatenate(
        [
            heads[..., :NOPE].reshape(rows, parts, -1),
            heads[..., NOPE:half].reshape(rows, parts, -1),
            heads[..., half:].reshape(rows, parts, -1),
        ],
        -1,
    )


def join_query(values, parts):
    rows = values.shape[0]
    own = HEADS // parts
    wide = own * NOPE
    narrow = own * (ROPE_D // 2)
    return jnp.concatenate(
        [
            values[..., :wide].reshape(rows, parts, own, NOPE),
            values[..., wide : wide + narrow].reshape(rows, parts, own, ROPE_D // 2),
            values[..., wide + narrow :].reshape(rows, parts, own, ROPE_D // 2),
        ],
        -1,
    ).reshape(rows, -1)


def split_up(weight, parts):
    rows = weight.shape[0]
    heads = weight.reshape(rows, parts, HEADS // parts, NOPE + VD)
    return jnp.concatenate(
        [heads[..., :NOPE].reshape(rows, parts, -1), heads[..., NOPE:].reshape(rows, parts, -1)], -1
    )


def join_up(values, parts):
    rows = values.shape[0]
    own = HEADS // parts
    return jnp.concatenate(
        [
            values[..., : own * NOPE].reshape(rows, parts, own, NOPE),
            values[..., own * NOPE :].reshape(rows, parts, own, VD),
        ],
        -1,
    ).reshape(rows, -1)


def swap_parts(pieces):
    ordered = by_part(pieces)
    return by_part([ordered[0]] + [hop(ordered[j], j) for j in range(1, 4)])


def gather_exp(pieces):
    full = lax.all_gather(jnp.stack(pieces), EXP, axis=1, tiled=True)
    return full.reshape(-1, full.shape[-1])


def to_heads(weight):
    return gather_exp(swap_parts([weight[:, j] for j in range(4)]))


def from_heads(grad, parts):
    experts = lax.axis_size(EXP)
    width = grad.shape[-1]
    full = grad.astype(BF).reshape(parts, experts, -1, width).transpose(1, 0, 2, 3)
    own = lax.psum_scatter(full.reshape(-1, width), EXP, scatter_dimension=0, tiled=True)
    own = own.reshape(parts, -1, width)
    return jnp.stack(swap_parts([own[a] for a in range(4)]), 1)


def shards(
    inputs,
    cotangent,
    expert_ids,
    attn_gain,
    query_weight,
    latent_down,
    latent_gain,
    latent_up,
    output_weight,
    ffn_gain,
    router_weight,
    shared_gate,
    shared_up,
    shared_down,
    expert_gate,
    expert_up,
    expert_down,
):
    parts = lax.axis_size(CTX)
    expert_devices = lax.axis_size(EXP)
    devices = parts * expert_devices
    my_part = lax.axis_index(CTX)
    my_expert = lax.axis_index(EXP)
    tok = inputs.shape[1]
    width = inputs.shape[2]
    group = tok * parts
    total = tok * devices
    rows = query_weight.shape[0]
    lat_rows = latent_gain.shape[0]
    expert_count = router_weight.shape[1]
    own_heads = HEADS // parts
    half = ROPE_D // 2
    low_width = KVR + ROPE_D
    attn_scale = 1.0 / math.sqrt(NOPE + ROPE_D)

    chosen = expert_ids[0]
    mask_own = jnp.sum(
        (chosen[:, :, None] == jnp.arange(expert_count)[None, None, :]).astype(F32), 1
    )
    mask_cols = tok * expert_count // rows
    pack_used = low_width + expert_count + 3
    pack = jnp.concatenate(
        [
            latent_down,
            router_weight,
            attn_gain[:, None],
            ffn_gain[:, None],
            jnp.pad(latent_gain, (0, rows - lat_rows))[:, None],
            mask_own.astype(BF).reshape(rows, mask_cols),
        ],
        1,
    )
    pack = pad_columns(pack, up_to(pack_used + mask_cols, 128))
    pack_full = gather_exp(by_part([pack] + [hop(pack, j) for j in range(1, 4)]))
    group_in = gather_ctx(inputs[0])
    weight_down = pack_full[:, :low_width]
    weight_router = pack_full[:, low_width : low_width + expert_count]
    gain_attn = pack_full[:, low_width + expert_count].astype(F32)
    gain_ffn = pack_full[:, low_width + expert_count + 1].astype(F32)
    gain_latent = (
        pack_full[:, low_width + expert_count + 2]
        .reshape(devices, rows)[:, :lat_rows]
        .reshape(KVR)
        .astype(F32)
    )
    mask = pack_full[:, pack_used : pack_used + mask_cols].reshape(total, expert_count).astype(F32)

    weight_query = to_heads(split_query(query_weight, parts))
    weight_up = to_heads(split_up(latent_up, parts))
    weight_output = lax.all_gather(output_weight, EXP, axis=0, tiled=True)
    own_sgate, own_sup = (
        lax.all_to_all(shared_gate, ALL, split_axis=1, concat_axis=0, tiled=True),
        lax.all_to_all(shared_up, ALL, split_axis=1, concat_axis=0, tiled=True),
    )
    chunks = max(1, total // 4096)

    early = chunks == 1 and lax.axis_size("chip") == 4

    group_rows = jnp.arange(group)
    place = place_of(my_part ^ (group_rows // tok), group_rows % tok, P_DEV * parts)
    allowed = place[None, :] <= place[:, None]
    cosine, sine = rotation(place, ROPE_D)
    cos_heads = jnp.tile(cosine, (1, own_heads))
    sin_heads = jnp.tile(sine, (1, own_heads))
    group_tokens = group_in.astype(F32)
    inv_root = lax.rsqrt(jnp.mean(group_tokens * group_tokens, -1, keepdims=True) + EPS)
    normed = (group_tokens * inv_root * gain_attn).astype(BF)
    if early:
        normed, cot_line = lax.optimization_barrier((normed, gather_line(cotangent[0])))
    query_raw = mm(normed, weight_query)
    wide = own_heads * NOPE
    narrow = own_heads * half
    query_nope = query_raw[:, :wide].astype(BF)
    query_first = query_raw[:, wide : wide + narrow]
    query_second = query_raw[:, wide + narrow :]
    turned_first = (query_first * cos_heads - query_second * sin_heads).astype(BF)
    turned_second = (query_first * sin_heads + query_second * cos_heads).astype(BF)
    query_rot = jnp.stack(
        [
            jnp.concatenate(
                [
                    query_nope[:, h * NOPE : (h + 1) * NOPE],
                    turned_first[:, h * half : (h + 1) * half],
                    turned_second[:, h * half : (h + 1) * half],
                ],
                1,
            )
            for h in range(own_heads)
        ]
    )
    latent_raw = mm(normed, weight_down)
    compressed = latent_raw[:, :KVR]
    latent_root = lax.rsqrt(jnp.mean(compressed * compressed, -1, keepdims=True) + EPS)
    latent_hat = compressed * latent_root
    latent_norm = (latent_hat * gain_latent).astype(BF)
    rope_first = latent_raw[:, KVR : KVR + half]
    rope_second = latent_raw[:, KVR + half :]
    key_rope = jnp.concatenate(
        [rope_first * cosine - rope_second * sine, rope_first * sine + rope_second * cosine], 1
    ).astype(BF)
    key_value = mm(latent_norm, weight_up).astype(BF)
    keys = jnp.stack(
        [
            jnp.concatenate([key_value[:, h * NOPE : (h + 1) * NOPE], key_rope], 1)
            for h in range(own_heads)
        ]
    )
    values = jnp.stack(
        [key_value[:, wide + h * VD : wide + (h + 1) * VD] for h in range(own_heads)]
    )
    scores = jnp.einsum("htd,hsd->hts", query_rot, keys, preferred_element_type=F32) * attn_scale
    scores = jnp.where(allowed[None], scores, -1e30)
    exp_scores = jnp.exp(scores - jnp.max(scores, -1, keepdims=True))
    probs = exp_scores / jnp.sum(exp_scores, -1, keepdims=True)
    weights_low = probs.astype(BF)
    attended = (
        jnp.einsum("hts,hsd->thd", weights_low, values, preferred_element_type=F32)
        .astype(BF)
        .reshape(group, own_heads * VD)
    )
    if early:
        attended, cot_pieces = lax.optimization_barrier((attended, gather_plane(cot_line)))
    projected = scatter_ctx(mm(attended, weight_output).astype(BF))
    tokens = inputs[0].astype(F32)
    hidden = tokens + projected
    inv_mid = lax.rsqrt(jnp.mean(hidden * hidden, -1, keepdims=True) + EPS)
    hidden_hat = hidden * inv_mid
    mixed = (hidden_hat * gain_ffn).astype(BF)

    exp_local, _, ff_own = expert_gate.shape
    routed = exp_local * ff_own
    own_units = routed + own_sgate.shape[1]
    weight_in = jnp.concatenate(
        [expert_gate[i] for i in range(exp_local)]
        + [own_sgate]
        + [expert_up[i] for i in range(exp_local)]
        + [own_sup, weight_router],
        1,
    )
    weight_out = jnp.concatenate([expert_down.reshape(routed, width), shared_down], 0)
    first_expert = my_expert * exp_local

    def run_units(all_mixed, all_cot, mask):
        count = all_mixed.shape[0]
        activations = mm(all_mixed, weight_in)
        gate_activation = activations[:, :own_units]
        up_activation = activations[:, own_units : 2 * own_units]
        probs_all = jax.nn.softmax(activations[:, 2 * own_units :], axis=-1)
        gates_local = lax.dynamic_slice(probs_all * mask, (0, first_expert), (count, exp_local))
        mask_local = lax.dynamic_slice(mask, (0, first_expert), (count, exp_local))
        gate_columns = jnp.concatenate(
            [jnp.broadcast_to(gates_local[:, i : i + 1], (count, ff_own)) for i in range(exp_local)]
            + [jnp.ones((count, own_units - routed), F32)],
            1,
        )
        sigma = jax.nn.sigmoid(gate_activation)
        gated = gate_activation * sigma
        unit = (gated * up_activation).astype(BF).astype(F32)
        scaled_unit = (unit * gate_columns).astype(BF)
        out_part = mm(scaled_unit, weight_out).astype(BF)
        grad_unit_raw = mm_nt(all_cot, weight_out)
        grad_gate_terms = grad_unit_raw * unit
        grad_gates = (
            jnp.concatenate(
                [
                    jnp.sum(grad_gate_terms[:, i * ff_own : (i + 1) * ff_own], 1, keepdims=True)
                    for i in range(exp_local)
                ],
                1,
            )
            * mask_local
        )
        grad_probs_part = lax.dynamic_update_slice(
            jnp.zeros((count, up_to(expert_count, 128)), F32), grad_gates, (0, first_expert)
        ).astype(BF)
        grad_unit = grad_unit_raw * gate_columns
        grad_gate_act = (
            grad_unit * up_activation * sigma * (1.0 + gate_activation * (1.0 - sigma))
        ).astype(BF)
        grad_up_act = (grad_unit * gated).astype(BF)
        grad_acts = jnp.concatenate([grad_gate_act, grad_up_act], 1)
        grad_mixed_part = mm_nt(grad_acts, weight_in[:, : 2 * own_units]).astype(BF)
        pair_grads = tuple(
            mm_tn(all_mixed, grad[:, i * ff_own : (i + 1) * ff_own])
            for grad in (grad_gate_act, grad_up_act)
            for i in range(exp_local)
        )
        back, (out_part, routed_grads, shared_grads) = scatter_tokens(
            jnp.concatenate([grad_mixed_part, grad_probs_part], 1),
            (
                out_part,
                (pair_grads, mm_tn(scaled_unit, all_cot)),
                tuple(
                    mm_tn(all_mixed, grad[:, routed:]).astype(BF)
                    for grad in (grad_gate_act, grad_up_act)
                ),
            ),
        )
        out_sum = scatter_all(out_part)
        weight_grads = (routed_grads[0], *shared_grads, routed_grads[1])
        return out_sum, back, weight_grads

    mask_tokens = mask.reshape(devices, tok, expert_count)
    runs = []
    for i in range(chunks):
        span = slice(i * tok // chunks, (i + 1) * tok // chunks)
        own_mixed, own_cot = mixed[span], cotangent[0, span]
        if runs:
            own_mixed, own_cot, _ = lax.optimization_barrier((own_mixed, own_cot, runs[-1][:2]))
        runs.append(
            run_units(
                gather_all(own_mixed),
                gather_cores(cot_pieces) if early else gather_all(own_cot),
                mask_tokens[:, span].reshape(-1, expert_count),
            )
        )
    out_sum = jnp.concatenate([r[0] for r in runs], 0).astype(F32)
    back = jnp.concatenate([r[1] for r in runs], 0)
    pair_grads, grad_sgate, grad_sup, grad_down_all = jax.tree.map(
        lambda *terms: sum(terms[1:], terms[0].astype(F32)), *[r[2] for r in runs]
    )
    expert_gate_total = jnp.stack(pair_grads[:exp_local])
    expert_up_total = jnp.stack(pair_grads[exp_local:])
    expert_down_total = grad_down_all[:routed].reshape(exp_local, ff_own, width)
    sum_sdown = grad_down_all[routed:]
    sum_sgate, sum_sup = (
        lax.all_to_all(
            grad_sgate.astype(BF), ALL, split_axis=0, concat_axis=1, tiled=True
        ).astype(F32),
        lax.all_to_all(grad_sup.astype(BF), ALL, split_axis=0, concat_axis=1, tiled=True).astype(
            F32
        ),
    )

    grad_probs = back[:, width : width + expert_count]
    router_probs = jax.nn.softmax(mm(mixed, weight_router), axis=-1)
    grad_logits = (
        router_probs * (grad_probs - jnp.sum(router_probs * grad_probs, -1, keepdims=True))
    ).astype(BF)
    grad_router = mm_tn(mixed, grad_logits)
    grad_mixed = back[:, :width] + mm_nt(grad_logits, weight_router)
    grad_mid, grad_gain_ffn = norm_back(grad_mixed, hidden_hat, inv_mid, gain_ffn)
    grad_hidden = cotangent[0].astype(F32) + grad_mid
    grad_proj = gather_ctx(grad_hidden.astype(BF))
    grad_output = mm_tn(attended, grad_proj).astype(BF)
    grad_att = mm_nt(grad_proj, weight_output).astype(BF)
    grad_att = jnp.stack([grad_att[:, h * VD : (h + 1) * VD] for h in range(own_heads)])
    grad_weights = jnp.einsum("htd,hsd->hts", grad_att, values, preferred_element_type=F32)
    grad_values = jnp.einsum("hts,htd->shd", weights_low, grad_att, preferred_element_type=F32)
    grad_scores = (
        probs * (grad_weights - jnp.sum(probs * grad_weights, -1, keepdims=True))
    ).astype(BF)
    grad_query = (
        jnp.einsum("hts,hsd->htd", grad_scores, keys, preferred_element_type=F32) * attn_scale
    )
    grad_keys = (
        jnp.einsum("hts,htd->hsd", grad_scores, query_rot, preferred_element_type=F32) * attn_scale
    )
    grad_first = jnp.concatenate(
        [grad_query[h, :, NOPE : NOPE + half] for h in range(own_heads)], 1
    )
    grad_second = jnp.concatenate([grad_query[h, :, NOPE + half :] for h in range(own_heads)], 1)
    grad_qraw = jnp.concatenate(
        [grad_query[h, :, :NOPE] for h in range(own_heads)]
        + [
            grad_first * cos_heads + grad_second * sin_heads,
            grad_second * cos_heads - grad_first * sin_heads,
        ],
        1,
    ).astype(BF)
    grad_kv = jnp.concatenate(
        [grad_keys[h, :, :NOPE] for h in range(own_heads)]
        + [grad_values.reshape(group, own_heads * VD)],
        1,
    ).astype(BF)
    grad_low = jnp.concatenate(
        [mm_nt(grad_kv, weight_up), jnp.sum(grad_keys[:, :, NOPE:], 0)], 1
    )
    grad_low = scatter_ctx(pad_columns(grad_low.astype(BF), up_to(low_width, 128)))
    grad_front = scatter_ctx(mm_nt(grad_qraw, weight_query).astype(BF))
    head_grads = (mm_tn(normed, grad_qraw).astype(BF), mm_tn(latent_norm, grad_kv).astype(BF))
    head_grads, grad_output, out_sum = lax.optimization_barrier((head_grads, grad_output, out_sum))
    sum_output = lax.psum_scatter(
        grad_output, EXP, scatter_dimension=0, tiled=True
    ).astype(F32)
    sum_query = join_query(from_heads(head_grads[0], parts), parts).astype(F32)
    sum_up = join_up(from_heads(head_grads[1], parts), parts).astype(F32)

    def own(values):
        return values[:tok]

    cos_own, sin_own = own(cosine), own(sine)
    grad_comp, grad_gain_latent = norm_back(
        grad_low[:, :KVR], own(latent_hat), own(latent_root), gain_latent
    )
    rope_grad_first = grad_low[:, KVR : KVR + half]
    rope_grad_second = grad_low[:, KVR + half : low_width]
    grad_lraw = jnp.concatenate(
        [
            grad_comp,
            rope_grad_first * cos_own + rope_grad_second * sin_own,
            rope_grad_second * cos_own - rope_grad_first * sin_own,
        ],
        1,
    ).astype(BF)
    lraw_group = gather_ctx(pad_columns(grad_lraw, up_to(low_width, 128)))[:, :low_width]
    block_rows = width // parts
    normed_block = lax.dynamic_slice_in_dim(normed, my_part * block_rows, block_rows, 1)
    grad_down = mm_tn(normed_block, lraw_group)
    grad_normed = grad_front + mm_nt(grad_lraw, weight_down)
    inv_own = own(inv_root)
    grad_entry, grad_gain_attn = norm_back(grad_normed, tokens * inv_own, inv_own, gain_attn)
    grad_inputs = grad_hidden + grad_entry

    small = jnp.concatenate(
        [
            grad_router,
            grad_gain_attn[:, None],
            grad_gain_ffn[:, None],
            jnp.pad(
                grad_gain_latent.reshape(devices, lat_rows), ((0, 0), (0, rows - lat_rows))
            ).reshape(width, 1),
        ],
        1,
    )
    small = pad_columns(small, up_to(pack_used, 128) - low_width).reshape(parts, block_rows, -1)
    small = by_part([small[a] for a in range(parts)])
    small = small[0] + sum(hop(small[j].astype(BF), j).astype(F32) for j in range(1, parts))
    pack_sum = scatter_exp(jnp.concatenate([grad_down, small], 1).astype(BF))
    return (
        (hidden + out_sum).astype(BF)[None],
        grad_inputs[None],
        pack_sum[:, low_width + expert_count],
        sum_query,
        pack_sum[:, :low_width],
        pack_sum[:lat_rows, low_width + expert_count + 2],
        sum_up,
        sum_output,
        pack_sum[:, low_width + expert_count + 1],
        pack_sum[:, low_width : low_width + expert_count],
        sum_sgate,
        sum_sup,
        sum_sdown,
        expert_gate_total,
        expert_up_total,
        expert_down_total,
    )


def solution(mesh):
    context, experts = mesh.devices.shape
    split = Mesh(mesh.devices.reshape(context, experts // 2, 2), ALL)
    tokens = P(EXP, CTX, None)
    dense = P(ALL, None)
    gain = P(ALL)
    columns = P(EXP, None, CTX)
    down = P(EXP, CTX, None)
    in_specs = (
        tokens, tokens, tokens, gain, dense, dense, gain, dense, dense, gain, dense, dense, dense,
        dense, columns, columns, down,
    )
    out_specs = (
        tokens, tokens, gain, dense, dense, gain, dense, dense, gain, dense, dense, dense, dense,
        columns, columns, down,
    )
    return jax.shard_map(shards, mesh=split, in_specs=in_specs, out_specs=out_specs, check_vma=False)
```

```python
import math

import jax
import jax.numpy as jnp
from jax import lax
from jax.sharding import Mesh
from jax.sharding import PartitionSpec as P


HEADS = 16
NOPE = 128
ROPE_D = 64
VD = 128
KVR = 512
P_DEV = 64
C_DEV = 64
EPS = 1e-06

CTX = "context"
EXP = ("chip", "core")
ALL = ("context", "chip", "core")
BF = jnp.bfloat16
F32 = jnp.float32


def mm(left, right):
    return lax.dot_general(left, right, (((1,), (0,)), ((), ())), preferred_element_type=F32)


def mm_tn(left, right):
    return lax.dot_general(left, right, (((0,), (0,)), ((), ())), preferred_element_type=F32)


def mm_nt(left, right):
    return lax.dot_general(left, right, (((1,), (1,)), ((), ())), preferred_element_type=F32)


def rotation(position, width):
    half = width // 2
    freqs = 10000.0 ** (-2.0 * jnp.arange(half).astype(F32) / width)
    angle = position.astype(F32)[:, None] * freqs[None, :]
    return (jnp.cos(angle), jnp.sin(angle))


def place_of(device, offset, prompt_total):
    return jnp.where(
        offset < P_DEV, device * P_DEV + offset, prompt_total + device * C_DEV + offset - P_DEV
    )


def norm_back(grad_out, normal, inv_root, gain):
    scaled = grad_out * gain
    grad_gain = jnp.sum(grad_out * normal, 0)
    grad_in = inv_root * (scaled - normal * jnp.mean(scaled * normal, -1, keepdims=True))
    return (grad_in, grad_gain)


def pad_columns(values, width):
    return jnp.pad(values, ((0, 0), (0, width - values.shape[1])))


def up_to(value, step):
    return -(-value // step) * step


def hop(values, flip):
    return lax.ppermute(values, CTX, [(i, i ^ flip) for i in range(4)])


def by_part(pieces):
    own = lax.axis_index(CTX)
    low = (own & 1) == 1
    high = (own & 2) == 2
    first = [jnp.where(low, pieces[a ^ 1], pieces[a]) for a in range(4)]
    return [jnp.where(high, first[a ^ 2], first[a]) for a in range(4)]


def gather_ctx(values):
    half = values.shape[0] // 2
    one = hop(values, 1)
    two = hop(values, 2)
    return jnp.concatenate([values, one, two, hop(two[:half], 1), hop(one[half:], 2)], 0)


def scatter_ctx(values):
    tok = values.shape[0] // 4
    return scatter_pieces([values[j * tok : (j + 1) * tok] for j in range(4)])


def scatter_pieces(pieces):
    half = pieces[0].shape[0] // 2
    head = [piece[:half] for piece in pieces]
    tail = [piece[half:] for piece in pieces]
    head_pass = hop(head[3], 1)
    tail_pass = hop(tail[3], 2)
    head_own = hop(head[1], 1)
    tail_own = hop(tail[2], 2)
    head_next = (head[2].astype(F32) + head_pass.astype(F32)).astype(BF)
    tail_next = (tail[1].astype(F32) + tail_pass.astype(F32)).astype(BF)
    head_last = hop(head_next, 2)
    tail_last = hop(tail_next, 1)
    return jnp.concatenate(
        [
            head[0].astype(F32) + head_own.astype(F32) + head_last.astype(F32),
            tail[0].astype(F32) + tail_own.astype(F32) + tail_last.astype(F32),
        ],
        0,
    )


def gather_all(values):
    return lax.all_gather(values, ALL, axis=0, tiled=True)


def scatter_all(values):
    return lax.psum_scatter(values, ALL, scatter_dimension=0, tiled=True)


def swap_core(values):
    return lax.ppermute(values, "core", [(0, 1), (1, 0)])


def shift_chip(values, step):
    return lax.ppermute(values, "chip", [(i, (i + step) % 4) for i in range(4)])


def put(target, values, *place):
    return lax.dynamic_update_slice(target, values, place + (0,) * (target.ndim - len(place)))


def gather_line(values):
    chip = lax.axis_index("chip")
    line = jnp.zeros((4,) + values.shape, values.dtype)
    for step in range(4):
        piece = shift_chip(values, step) if step else values
        line = put(line, piece[None], (chip - step) % 4)
    return line


def gather_plane(line):
    one = hop(line, 1)
    two = hop(line, 2)
    return [line, one, two, hop(two[:2], 1), hop(one[2:], 2)]


def gather_cores(pieces):
    _, tok, width = pieces[0].shape
    part, _, core = (lax.axis_index(a) for a in ALL)
    full = jnp.zeros((4, 4, 2, tok, width), pieces[0].dtype)
    for piece, flip, first in zip(pieces, (0, 1, 2, 3, 3), (0, 0, 0, 0, 2)):
        other = swap_core(piece)
        full = put(full, piece[None, :, None], part ^ flip, first, core)
        full = put(full, other[None, :, None], part ^ flip, first, 1 - core)
    return full.reshape(-1, width)


def scatter_line(values, axis_values):
    chip = lax.axis_index("chip")
    total = lax.dynamic_index_in_dim(values, chip, 0, False)
    for step in range(1, 4):
        block = lax.dynamic_index_in_dim(axis_values, (chip + step) % 4, 0, False)
        total = total + shift_chip(block, step).astype(F32)
    return total


def add_cores(blocks):
    core = lax.axis_index("core")
    axis = blocks.ndim - 3
    away = swap_core(lax.dynamic_index_in_dim(blocks, 1 - core, axis, False))
    return lax.dynamic_index_in_dim(blocks, core, axis, False).astype(F32) + away.astype(F32)


def scatter_cores(values):
    part, _, core = (lax.axis_index(a) for a in ALL)
    tok = values[0].shape[0] // 32

    def rows(flip, side):
        return jnp.concatenate(
            [
                jnp.concatenate(
                    [
                        lax.dynamic_slice_in_dim(
                            value, (((part ^ flip) * 4 + chip) * 2 + side) * tok, tok, 0
                        )
                        for value in values
                    ],
                    1,
                )
                for chip in range(4)
            ],
            0,
        )

    away = [swap_core(rows(flip, 1 - core)) for flip in range(4)]
    return [
        (rows(flip, core).astype(F32) + away[flip].astype(F32)).astype(BF) for flip in range(4)
    ]


def scatter_rest(sums, beside):
    own, beside = lax.optimization_barrier((scatter_pieces(sums), beside))
    chip = lax.axis_index("chip")
    tok = own.shape[0] // 4
    total = lax.dynamic_slice_in_dim(own, chip * tok, tok, 0)
    low = own.astype(BF)
    for step in range(1, 4):
        block = lax.dynamic_slice_in_dim(low, (chip + step) % 4 * tok, tok, 0)
        total = total + shift_chip(block, step).astype(F32)
    return total, beside


def scatter_exp(values):
    if lax.axis_size("chip") != 4:
        return lax.psum_scatter(values, EXP, scatter_dimension=0, tiled=True).astype(F32)
    own = add_cores(values.reshape(4, 2, -1, values.shape[1]))
    return scatter_line(own, own.astype(BF))


def split_query(weight, parts):
    rows = weight.shape[0]
    heads = weight.reshape(rows, parts, HEADS // parts, NOPE + ROPE_D)
    half = NOPE + ROPE_D // 2
    return jnp.concatenate(
        [
            heads[..., :NOPE].reshape(rows, parts, -1),
            heads[..., NOPE:half].reshape(rows, parts, -1),
            heads[..., half:].reshape(rows, parts, -1),
        ],
        -1,
    )


def join_query(values, parts):
    rows = values.shape[0]
    own = HEADS // parts
    wide = own * NOPE
    narrow = own * (ROPE_D // 2)
    return jnp.concatenate(
        [
            values[..., :wide].reshape(rows, parts, own, NOPE),
            values[..., wide : wide + narrow].reshape(rows, parts, own, ROPE_D // 2),
            values[..., wide + narrow :].reshape(rows, parts, own, ROPE_D // 2),
        ],
        -1,
    ).reshape(rows, -1)


def split_up(weight, parts):
    rows = weight.shape[0]
    heads = weight.reshape(rows, parts, HEADS // parts, NOPE + VD)
    return jnp.concatenate(
        [heads[..., :NOPE].reshape(rows, parts, -1), heads[..., NOPE:].reshape(rows, parts, -1)], -1
    )


def join_up(values, parts):
    rows = values.shape[0]
    own = HEADS // parts
    return jnp.concatenate(
        [
            values[..., : own * NOPE].reshape(rows, parts, own, NOPE),
            values[..., own * NOPE :].reshape(rows, parts, own, VD),
        ],
        -1,
    ).reshape(rows, -1)


def swap_parts(pieces):
    ordered = by_part(pieces)
    return by_part([ordered[0]] + [hop(ordered[j], j) for j in range(1, 4)])


def gather_exp(pieces):
    full = lax.all_gather(jnp.stack(pieces), EXP, axis=1, tiled=True)
    return full.reshape(-1, full.shape[-1])


def to_heads(weight):
    return gather_exp(swap_parts([weight[:, j] for j in range(4)]))


def from_heads(grad, parts):
    experts = lax.axis_size(EXP)
    width = grad.shape[-1]
    full = grad.astype(BF).reshape(parts, experts, -1, width).transpose(1, 0, 2, 3)
    own = lax.psum_scatter(full.reshape(-1, width), EXP, scatter_dimension=0, tiled=True)
    own = own.reshape(parts, -1, width)
    return jnp.stack(swap_parts([own[a] for a in range(4)]), 1)


def shards(
    inputs,
    cotangent,
    expert_ids,
    attn_gain,
    query_weight,
    latent_down,
    latent_gain,
    latent_up,
    output_weight,
    ffn_gain,
    router_weight,
    shared_gate,
    shared_up,
    shared_down,
    expert_gate,
    expert_up,
    expert_down,
):
    parts = lax.axis_size(CTX)
    expert_devices = lax.axis_size(EXP)
    devices = parts * expert_devices
    my_part = lax.axis_index(CTX)
    my_expert = lax.axis_index(EXP)
    tok = inputs.shape[1]
    width = inputs.shape[2]
    group = tok * parts
    total = tok * devices
    rows = query_weight.shape[0]
    lat_rows = latent_gain.shape[0]
    expert_count = router_weight.shape[1]
    own_heads = HEADS // parts
    half = ROPE_D // 2
    low_width = KVR + ROPE_D
    attn_scale = 1.0 / math.sqrt(NOPE + ROPE_D)

    chosen = expert_ids[0]
    mask_own = jnp.sum(
        (chosen[:, :, None] == jnp.arange(expert_count)[None, None, :]).astype(F32), 1
    )
    mask_cols = tok * expert_count // rows
    pack_used = low_width + expert_count + 3
    pack = jnp.concatenate(
        [
            latent_down,
            router_weight,
            attn_gain[:, None],
            ffn_gain[:, None],
            jnp.pad(latent_gain, (0, rows - lat_rows))[:, None],
            mask_own.astype(BF).reshape(rows, mask_cols),
        ],
        1,
    )
    pack = pad_columns(pack, up_to(pack_used + mask_cols, 128))
    pack_full = gather_exp(by_part([pack] + [hop(pack, j) for j in range(1, 4)]))
    group_in = gather_ctx(inputs[0])
    weight_down = pack_full[:, :low_width]
    weight_router = pack_full[:, low_width : low_width + expert_count]
    gain_attn = pack_full[:, low_width + expert_count].astype(F32)
    gain_ffn = pack_full[:, low_width + expert_count + 1].astype(F32)
    gain_latent = (
        pack_full[:, low_width + expert_count + 2]
        .reshape(devices, rows)[:, :lat_rows]
        .reshape(KVR)
        .astype(F32)
    )
    mask = pack_full[:, pack_used : pack_used + mask_cols].reshape(total, expert_count).astype(F32)

    weight_query = to_heads(split_query(query_weight, parts))
    weight_up = to_heads(split_up(latent_up, parts))
    weight_output = lax.all_gather(output_weight, EXP, axis=0, tiled=True)
    own_shared = lax.all_to_all(
        jnp.concatenate(
            [w.reshape(rows, devices, 1, -1) for w in (shared_gate, shared_up)], 2
        ).reshape(rows, -1),
        ALL, split_axis=1, concat_axis=0, tiled=True,
    )
    own_sgate, own_sup = jnp.split(own_shared, 2, axis=1)
    chunks = max(1, total // 4096)

    early = chunks == 1 and lax.axis_size("chip") == 4

    group_rows = jnp.arange(group)
    place = place_of(my_part ^ (group_rows // tok), group_rows % tok, P_DEV * parts)
    allowed = place[None, :] <= place[:, None]
    cosine, sine = rotation(place, ROPE_D)
    cos_heads = jnp.tile(cosine, (1, own_heads))
    sin_heads = jnp.tile(sine, (1, own_heads))
    group_tokens = group_in.astype(F32)
    inv_root = lax.rsqrt(jnp.mean(group_tokens * group_tokens, -1, keepdims=True) + EPS)
    normed = (group_tokens * inv_root * gain_attn).astype(BF)
    if early:
        normed, cot_line = lax.optimization_barrier((normed, gather_line(cotangent[0])))
    query_raw = mm(normed, weight_query)
    wide = own_heads * NOPE
    narrow = own_heads * half
    query_nope = query_raw[:, :wide].astype(BF)
    query_first = query_raw[:, wide : wide + narrow]
    query_second = query_raw[:, wide + narrow :]
    turned_first = (query_first * cos_heads - query_second * sin_heads).astype(BF)
    turned_second = (query_first * sin_heads + query_second * cos_heads).astype(BF)
    query_rot = jnp.stack(
        [
            jnp.concatenate(
                [
                    query_nope[:, h * NOPE : (h + 1) * NOPE],
                    turned_first[:, h * half : (h + 1) * half],
                    turned_second[:, h * half : (h + 1) * half],
                ],
                1,
            )
            for h in range(own_heads)
        ]
    )
    latent_raw = mm(normed, weight_down)
    compressed = latent_raw[:, :KVR]
    latent_root = lax.rsqrt(jnp.mean(compressed * compressed, -1, keepdims=True) + EPS)
    latent_hat = compressed * latent_root
    latent_norm = (latent_hat * gain_latent).astype(BF)
    rope_first = latent_raw[:, KVR : KVR + half]
    rope_second = latent_raw[:, KVR + half :]
    key_rope = jnp.concatenate(
        [rope_first * cosine - rope_second * sine, rope_first * sine + rope_second * cosine], 1
    ).astype(BF)
    key_value = mm(latent_norm, weight_up).astype(BF)
    keys = jnp.stack(
        [
            jnp.concatenate([key_value[:, h * NOPE : (h + 1) * NOPE], key_rope], 1)
            for h in range(own_heads)
        ]
    )
    values = jnp.stack(
        [key_value[:, wide + h * VD : wide + (h + 1) * VD] for h in range(own_heads)]
    )
    scores = jnp.einsum("htd,hsd->hts", query_rot, keys, preferred_element_type=F32) * attn_scale
    scores = jnp.where(allowed[None], scores, -1e30)
    exp_scores = jnp.exp(scores - jnp.max(scores, -1, keepdims=True))
    probs = exp_scores / jnp.sum(exp_scores, -1, keepdims=True)
    weights_low = probs.astype(BF)
    attended = (
        jnp.einsum("hts,hsd->thd", weights_low, values, preferred_element_type=F32)
        .astype(BF)
        .reshape(group, own_heads * VD)
    )
    if early:
        attended, cot_pieces = lax.optimization_barrier((attended, gather_plane(cot_line)))
    projected = scatter_ctx(mm(attended, weight_output).astype(BF))
    tokens = inputs[0].astype(F32)
    hidden = tokens + projected
    inv_mid = lax.rsqrt(jnp.mean(hidden * hidden, -1, keepdims=True) + EPS)
    hidden_hat = hidden * inv_mid
    mixed = (hidden_hat * gain_ffn).astype(BF)

    exp_local, _, ff_own = expert_gate.shape
    routed = exp_local * ff_own
    own_units = routed + own_sgate.shape[1]
    weight_in = jnp.concatenate(
        [expert_gate[i] for i in range(exp_local)]
        + [own_sgate]
        + [expert_up[i] for i in range(exp_local)]
        + [own_sup, weight_router],
        1,
    )
    weight_out = jnp.concatenate([expert_down.reshape(routed, width), shared_down], 0)
    first_expert = my_expert * exp_local

    def run_units(all_mixed, all_cot, mask):
        count = all_mixed.shape[0]
        activations = mm(all_mixed, weight_in)
        gate_activation = activations[:, :own_units]
        up_activation = activations[:, own_units : 2 * own_units]
        probs_all = jax.nn.softmax(activations[:, 2 * own_units :], axis=-1)
        gates_local = lax.dynamic_slice(probs_all * mask, (0, first_expert), (count, exp_local))
        mask_local = lax.dynamic_slice(mask, (0, first_expert), (count, exp_local))
        gate_columns = jnp.concatenate(
            [jnp.broadcast_to(gates_local[:, i : i + 1], (count, ff_own)) for i in range(exp_local)]
            + [jnp.ones((count, own_units - routed), F32)],
            1,
        )
        sigma = jax.nn.sigmoid(gate_activation)
        gated = gate_activation * sigma
        unit = (gated * up_activation).astype(BF).astype(F32)
        scaled_unit = (unit * gate_columns).astype(BF)
        grad_unit_raw = mm_nt(all_cot, weight_out)
        grad_gate_terms = grad_unit_raw * unit
        grad_gates = (
            jnp.concatenate(
                [
                    jnp.sum(grad_gate_terms[:, i * ff_own : (i + 1) * ff_own], 1, keepdims=True)
                    for i in range(exp_local)
                ],
                1,
            )
            * mask_local
        )
        grad_probs_part = lax.dynamic_update_slice(
            jnp.zeros((count, up_to(expert_count, 128)), F32), grad_gates, (0, first_expert)
        ).astype(BF)
        grad_unit = grad_unit_raw * gate_columns
        grad_gate_act = (
            grad_unit * up_activation * sigma * (1.0 + gate_activation * (1.0 - sigma))
        ).astype(BF)
        grad_up_act = (grad_unit * gated).astype(BF)
        grad_acts = jnp.concatenate([grad_gate_act, grad_up_act], 1)
        grad_mixed_part = mm_nt(grad_acts, weight_in[:, : 2 * own_units]).astype(BF)
        line = lax.axis_size("chip") == 4
        if line:
            grad_mixed_part, scaled_unit = lax.optimization_barrier((grad_mixed_part, scaled_unit))
            sums = scatter_cores([grad_mixed_part, grad_probs_part])
        out_part = mm(scaled_unit, weight_out).astype(BF)
        if line:
            sums, out_part, all_mixed, all_cot = lax.optimization_barrier(
                (sums, out_part, all_mixed, all_cot)
            )
        pair_grads = tuple(
            mm_tn(all_mixed, grad[:, i * ff_own : (i + 1) * ff_own])
            for grad in (grad_gate_act, grad_up_act)
            for i in range(exp_local)
        )
        routed_grads = (pair_grads, mm_tn(scaled_unit, all_cot))
        shared_grads = mm_tn(
            all_mixed, jnp.concatenate([grad_gate_act[:, routed:], grad_up_act[:, routed:]], 1)
        ).astype(BF)
        if line:
            out_sums = scatter_cores([out_part])
            back, (out_sums, routed_grads, shared_grads) = scatter_rest(
                sums, (out_sums, routed_grads, shared_grads)
            )
            out_sum, _ = scatter_rest(out_sums, ())
        else:
            back = scatter_all(jnp.concatenate([grad_mixed_part, grad_probs_part], 1)).astype(F32)
            out_sum = scatter_all(out_part)
        weight_grads = (routed_grads[0], shared_grads, routed_grads[1])
        return out_sum, back, weight_grads

    mask_tokens = mask.reshape(devices, tok, expert_count)
    runs = []
    for i in range(chunks):
        span = slice(i * tok // chunks, (i + 1) * tok // chunks)
        own_mixed, own_cot = mixed[span], cotangent[0, span]
        if runs:
            own_mixed, own_cot, _ = lax.optimization_barrier((own_mixed, own_cot, runs[-1][:2]))
        runs.append(
            run_units(
                gather_all(own_mixed),
                gather_cores(cot_pieces) if early else gather_all(own_cot),
                mask_tokens[:, span].reshape(-1, expert_count),
            )
        )
    out_sum = jnp.concatenate([r[0] for r in runs], 0).astype(F32)
    back = jnp.concatenate([r[1] for r in runs], 0)
    pair_grads, grad_shared, grad_down_all = jax.tree.map(
        lambda *terms: sum(terms[1:], terms[0].astype(F32)), *[r[2] for r in runs]
    )
    expert_gate_total = jnp.stack(pair_grads[:exp_local])
    expert_up_total = jnp.stack(pair_grads[exp_local:])
    expert_down_total = grad_down_all[:routed].reshape(exp_local, ff_own, width)
    sum_sdown = grad_down_all[routed:]
    sum_shared = lax.all_to_all(
        grad_shared.astype(BF), ALL, split_axis=0, concat_axis=1, tiled=True
    )

    grad_probs = back[:, width : width + expert_count]
    router_probs = jax.nn.softmax(mm(mixed, weight_router), axis=-1)
    grad_logits = (
        router_probs * (grad_probs - jnp.sum(router_probs * grad_probs, -1, keepdims=True))
    ).astype(BF)
    grad_router = mm_tn(mixed, grad_logits)
    grad_mixed = back[:, :width] + mm_nt(grad_logits, weight_router)
    grad_mid, grad_gain_ffn = norm_back(grad_mixed, hidden_hat, inv_mid, gain_ffn)
    grad_hidden = cotangent[0].astype(F32) + grad_mid
    grad_proj = gather_ctx(grad_hidden.astype(BF))
    grad_output = mm_tn(attended, grad_proj).astype(BF)
    grad_att = mm_nt(grad_proj, weight_output).astype(BF)
    grad_att = jnp.stack([grad_att[:, h * VD : (h + 1) * VD] for h in range(own_heads)])
    grad_weights = jnp.einsum("htd,hsd->hts", grad_att, values, preferred_element_type=F32)
    grad_values = jnp.einsum("hts,htd->shd", weights_low, grad_att, preferred_element_type=F32)
    grad_scores = (
        probs * (grad_weights - jnp.sum(probs * grad_weights, -1, keepdims=True))
    ).astype(BF)
    grad_query = (
        jnp.einsum("hts,hsd->htd", grad_scores, keys, preferred_element_type=F32) * attn_scale
    )
    grad_keys = (
        jnp.einsum("hts,htd->hsd", grad_scores, query_rot, preferred_element_type=F32) * attn_scale
    )
    grad_first = jnp.concatenate(
        [grad_query[h, :, NOPE : NOPE + half] for h in range(own_heads)], 1
    )
    grad_second = jnp.concatenate([grad_query[h, :, NOPE + half :] for h in range(own_heads)], 1)
    grad_qraw = jnp.concatenate(
        [grad_query[h, :, :NOPE] for h in range(own_heads)]
        + [
            grad_first * cos_heads + grad_second * sin_heads,
            grad_second * cos_heads - grad_first * sin_heads,
        ],
        1,
    ).astype(BF)
    grad_kv = jnp.concatenate(
        [grad_keys[h, :, :NOPE] for h in range(own_heads)]
        + [grad_values.reshape(group, own_heads * VD)],
        1,
    ).astype(BF)
    grad_low = jnp.concatenate(
        [mm_nt(grad_kv, weight_up), jnp.sum(grad_keys[:, :, NOPE:], 0)], 1
    )
    grad_low, sum_shared = lax.optimization_barrier((grad_low, sum_shared))
    sum_shared = sum_shared.astype(F32).reshape(rows, devices, 2, -1)
    sum_sgate, sum_sup = (sum_shared[:, :, i].reshape(rows, -1) for i in range(2))
    grad_low = scatter_ctx(pad_columns(grad_low.astype(BF), up_to(low_width, 128)))
    grad_front = scatter_ctx(mm_nt(grad_qraw, weight_query).astype(BF))
    head_grads = (mm_tn(normed, grad_qraw).astype(BF), mm_tn(latent_norm, grad_kv).astype(BF))
    sum_output = lax.psum_scatter(
        grad_output, EXP, scatter_dimension=0, tiled=True
    ).astype(F32)
    sum_query = join_query(from_heads(head_grads[0], parts), parts).astype(F32)
    sum_up = join_up(from_heads(head_grads[1], parts), parts).astype(F32)

    def own(values):
        return values[:tok]

    cos_own, sin_own = own(cosine), own(sine)
    grad_comp, grad_gain_latent = norm_back(
        grad_low[:, :KVR], own(latent_hat), own(latent_root), gain_latent
    )
    rope_grad_first = grad_low[:, KVR : KVR + half]
    rope_grad_second = grad_low[:, KVR + half : low_width]
    grad_lraw = jnp.concatenate(
        [
            grad_comp,
            rope_grad_first * cos_own + rope_grad_second * sin_own,
            rope_grad_second * cos_own - rope_grad_first * sin_own,
        ],
        1,
    ).astype(BF)
    lraw_group = gather_ctx(pad_columns(grad_lraw, up_to(low_width, 128)))[:, :low_width]
    block_rows = width // parts
    normed_block = lax.dynamic_slice_in_dim(normed, my_part * block_rows, block_rows, 1)
    grad_down = mm_tn(normed_block, lraw_group)
    grad_normed = grad_front + mm_nt(grad_lraw, weight_down)
    inv_own = own(inv_root)
    grad_entry, grad_gain_attn = norm_back(grad_normed, tokens * inv_own, inv_own, gain_attn)
    grad_inputs = grad_hidden + grad_entry

    small = jnp.concatenate(
        [
            grad_router,
            grad_gain_attn[:, None],
            grad_gain_ffn[:, None],
            jnp.pad(
                grad_gain_latent.reshape(devices, lat_rows), ((0, 0), (0, rows - lat_rows))
            ).reshape(width, 1),
        ],
        1,
    )
    small = pad_columns(small, up_to(pack_used, 128) - low_width).reshape(parts, block_rows, -1)
    small = by_part([small[a] for a in range(parts)])
    small = small[0] + sum(hop(small[j].astype(BF), j).astype(F32) for j in range(1, parts))
    pack_sum = scatter_exp(jnp.concatenate([grad_down, small], 1).astype(BF))
    return (
        (hidden + out_sum).astype(BF)[None],
        grad_inputs[None],
        pack_sum[:, low_width + expert_count],
        sum_query,
        pack_sum[:, :low_width],
        pack_sum[:lat_rows, low_width + expert_count + 2],
        sum_up,
        sum_output,
        pack_sum[:, low_width + expert_count + 1],
        pack_sum[:, low_width : low_width + expert_count],
        sum_sgate,
        sum_sup,
        sum_sdown,
        expert_gate_total,
        expert_up_total,
        expert_down_total,
    )


def solution(mesh):
    context, experts = mesh.devices.shape
    split = Mesh(mesh.devices.reshape(context, experts // 2, 2), ALL)
    tokens = P(EXP, CTX, None)
    dense = P(ALL, None)
    gain = P(ALL)
    columns = P(EXP, None, CTX)
    down = P(EXP, CTX, None)
    in_specs = (
        tokens, tokens, tokens, gain, dense, dense, gain, dense, dense, gain, dense, dense, dense,
        dense, columns, columns, down,
    )
    out_specs = (
        tokens, tokens, gain, dense, dense, gain, dense, dense, gain, dense, dense, dense, dense,
        columns, columns, down,
    )
    return jax.shard_map(
        shards, mesh=split, in_specs=in_specs, out_specs=out_specs, check_vma=False
    )
```

```python
import math

import jax
import jax.numpy as jnp
from jax import lax
from jax.sharding import Mesh
from jax.sharding import PartitionSpec as P


HEADS = 16
NOPE = 128
ROPE_D = 64
VD = 128
KVR = 512
P_DEV = 64
C_DEV = 64
EPS = 1e-06

CTX = "context"
EXP = ("chip", "core")
ALL = ("context", "chip", "core")
BF = jnp.bfloat16
F32 = jnp.float32


def mm(left, right):
    return lax.dot_general(left, right, (((1,), (0,)), ((), ())), preferred_element_type=F32)


def mm_tn(left, right):
    return lax.dot_general(left, right, (((0,), (0,)), ((), ())), preferred_element_type=F32)


def mm_nt(left, right):
    return lax.dot_general(left, right, (((1,), (1,)), ((), ())), preferred_element_type=F32)


def rotation(position, width):
    half = width // 2
    freqs = 10000.0 ** (-2.0 * jnp.arange(half).astype(F32) / width)
    angle = position.astype(F32)[:, None] * freqs[None, :]
    return (jnp.cos(angle), jnp.sin(angle))


def place_of(device, offset, prompt_total):
    return jnp.where(
        offset < P_DEV, device * P_DEV + offset, prompt_total + device * C_DEV + offset - P_DEV
    )


def norm_back(grad_out, normal, inv_root, gain):
    scaled = grad_out * gain
    grad_gain = jnp.sum(grad_out * normal, 0)
    grad_in = inv_root * (scaled - normal * jnp.mean(scaled * normal, -1, keepdims=True))
    return (grad_in, grad_gain)


def pad_columns(values, width):
    return jnp.pad(values, ((0, 0), (0, width - values.shape[1])))


def up_to(value, step):
    return -(-value // step) * step


def hop(values, flip):
    return lax.ppermute(values, CTX, [(i, i ^ flip) for i in range(4)])


def by_part(pieces):
    own = lax.axis_index(CTX)
    low = (own & 1) == 1
    high = (own & 2) == 2
    first = [jnp.where(low, pieces[a ^ 1], pieces[a]) for a in range(4)]
    return [jnp.where(high, first[a ^ 2], first[a]) for a in range(4)]


def gather_ctx(values):
    half = values.shape[0] // 2
    one = hop(values, 1)
    two = hop(values, 2)
    return jnp.concatenate([values, one, two, hop(two[:half], 1), hop(one[half:], 2)], 0)


def scatter_ctx(values):
    tok = values.shape[0] // 4
    return scatter_pieces([values[j * tok : (j + 1) * tok] for j in range(4)])


def scatter_pieces(pieces):
    half = pieces[0].shape[0] // 2
    head = [piece[:half] for piece in pieces]
    tail = [piece[half:] for piece in pieces]
    head_pass = hop(head[3], 1)
    tail_pass = hop(tail[3], 2)
    head_own = hop(head[1], 1)
    tail_own = hop(tail[2], 2)
    head_next = (head[2].astype(F32) + head_pass.astype(F32)).astype(BF)
    tail_next = (tail[1].astype(F32) + tail_pass.astype(F32)).astype(BF)
    head_last = hop(head_next, 2)
    tail_last = hop(tail_next, 1)
    return jnp.concatenate(
        [
            head[0].astype(F32) + head_own.astype(F32) + head_last.astype(F32),
            tail[0].astype(F32) + tail_own.astype(F32) + tail_last.astype(F32),
        ],
        0,
    )


def gather_all(values):
    return lax.all_gather(values, ALL, axis=0, tiled=True)


def scatter_all(values):
    return lax.psum_scatter(values, ALL, scatter_dimension=0, tiled=True)


def swap_core(values):
    return lax.ppermute(values, "core", [(0, 1), (1, 0)])


def shift_chip(values, step):
    return lax.ppermute(values, "chip", [(i, (i + step) % 4) for i in range(4)])


def put(target, values, *place):
    return lax.dynamic_update_slice(target, values, place + (0,) * (target.ndim - len(place)))


def gather_line(values):
    chip = lax.axis_index("chip")
    line = jnp.zeros((4,) + values.shape, values.dtype)
    for step in range(4):
        piece = shift_chip(values, step) if step else values
        line = put(line, piece[None], (chip - step) % 4)
    return line


def gather_plane(line):
    one = hop(line, 1)
    two = hop(line, 2)
    return [line, one, two, hop(two[:2], 1), hop(one[2:], 2)]


def gather_cores(pieces):
    _, tok, width = pieces[0].shape
    part, _, core = (lax.axis_index(a) for a in ALL)
    full = jnp.zeros((4, 4, 2, tok, width), pieces[0].dtype)
    for piece, flip, first in zip(pieces, (0, 1, 2, 3, 3), (0, 0, 0, 0, 2)):
        other = swap_core(piece)
        full = put(full, piece[None, :, None], part ^ flip, first, core)
        full = put(full, other[None, :, None], part ^ flip, first, 1 - core)
    return full.reshape(-1, width)


def scatter_line(values, axis_values):
    chip = lax.axis_index("chip")
    total = lax.dynamic_index_in_dim(values, chip, 0, False)
    for step in range(1, 4):
        block = lax.dynamic_index_in_dim(axis_values, (chip + step) % 4, 0, False)
        total = total + shift_chip(block, step).astype(F32)
    return total


def add_cores(blocks):
    core = lax.axis_index("core")
    axis = blocks.ndim - 3
    away = swap_core(lax.dynamic_index_in_dim(blocks, 1 - core, axis, False))
    return lax.dynamic_index_in_dim(blocks, core, axis, False).astype(F32) + away.astype(F32)


def scatter_cores(values):
    part, _, core = (lax.axis_index(a) for a in ALL)
    tok = values.shape[0] // 32

    def rows(flip, side):
        return jnp.concatenate(
            [
                lax.dynamic_slice_in_dim(
                    values, (((part ^ flip) * 4 + chip) * 2 + side) * tok, tok, 0
                )
                for chip in range(4)
            ],
            0,
        )

    away = [swap_core(rows(flip, 1 - core)) for flip in range(4)]
    return [
        (rows(flip, core).astype(F32) + away[flip].astype(F32)).astype(BF) for flip in range(4)
    ]


def scatter_rest(sums, beside):
    own, beside = lax.optimization_barrier((scatter_pieces(sums), beside))
    chip = lax.axis_index("chip")
    tok = own.shape[0] // 4
    total = lax.dynamic_slice_in_dim(own, chip * tok, tok, 0)
    low = own.astype(BF)
    for step in range(1, 4):
        block = lax.dynamic_slice_in_dim(low, (chip + step) % 4 * tok, tok, 0)
        moved = shift_chip(block, step)
        total = total + moved.astype(F32)
    return total, beside


def scatter_exp(values):
    if lax.axis_size("chip") != 4:
        return lax.psum_scatter(values, EXP, scatter_dimension=0, tiled=True).astype(F32)
    own = add_cores(values.reshape(4, 2, -1, values.shape[1]))
    return scatter_line(own, own.astype(BF))


def split_query(weight, parts):
    rows = weight.shape[0]
    heads = weight.reshape(rows, parts, HEADS // parts, NOPE + ROPE_D)
    half = NOPE + ROPE_D // 2
    return jnp.concatenate(
        [
            heads[..., :NOPE].reshape(rows, parts, -1),
            heads[..., NOPE:half].reshape(rows, parts, -1),
            heads[..., half:].reshape(rows, parts, -1),
        ],
        -1,
    )


def join_query(values, parts):
    rows = values.shape[0]
    own = HEADS // parts
    wide = own * NOPE
    narrow = own * (ROPE_D // 2)
    return jnp.concatenate(
        [
            values[..., :wide].reshape(rows, parts, own, NOPE),
            values[..., wide : wide + narrow].reshape(rows, parts, own, ROPE_D // 2),
            values[..., wide + narrow :].reshape(rows, parts, own, ROPE_D // 2),
        ],
        -1,
    ).reshape(rows, -1)


def split_up(weight, parts):
    rows = weight.shape[0]
    heads = weight.reshape(rows, parts, HEADS // parts, NOPE + VD)
    return jnp.concatenate(
        [heads[..., :NOPE].reshape(rows, parts, -1), heads[..., NOPE:].reshape(rows, parts, -1)], -1
    )


def join_up(values, parts):
    rows = values.shape[0]
    own = HEADS // parts
    return jnp.concatenate(
        [
            values[..., : own * NOPE].reshape(rows, parts, own, NOPE),
            values[..., own * NOPE :].reshape(rows, parts, own, VD),
        ],
        -1,
    ).reshape(rows, -1)


def swap_parts(pieces):
    ordered = by_part(pieces)
    return by_part([ordered[0]] + [hop(ordered[j], j) for j in range(1, 4)])


def gather_exp(pieces):
    full = lax.all_gather(jnp.stack(pieces), EXP, axis=1, tiled=True)
    return full.reshape(-1, full.shape[-1])


def to_heads(weight):
    return gather_exp(swap_parts([weight[:, j] for j in range(4)]))


def from_heads(grad, parts):
    experts = lax.axis_size(EXP)
    width = grad.shape[-1]
    full = grad.astype(BF).reshape(parts, experts, -1, width).transpose(1, 0, 2, 3)
    own = lax.psum_scatter(full.reshape(-1, width), EXP, scatter_dimension=0, tiled=True)
    own = own.reshape(parts, -1, width)
    return jnp.stack(swap_parts([own[a] for a in range(4)]), 1)


def shards(
    inputs,
    cotangent,
    expert_ids,
    attn_gain,
    query_weight,
    latent_down,
    latent_gain,
    latent_up,
    output_weight,
    ffn_gain,
    router_weight,
    shared_gate,
    shared_up,
    shared_down,
    expert_gate,
    expert_up,
    expert_down,
):
    parts = lax.axis_size(CTX)
    expert_devices = lax.axis_size(EXP)
    devices = parts * expert_devices
    my_part = lax.axis_index(CTX)
    my_expert = lax.axis_index(EXP)
    tok = inputs.shape[1]
    width = inputs.shape[2]
    group = tok * parts
    total = tok * devices
    rows = query_weight.shape[0]
    lat_rows = latent_gain.shape[0]
    expert_count = router_weight.shape[1]
    own_heads = HEADS // parts
    half = ROPE_D // 2
    low_width = KVR + ROPE_D
    attn_scale = 1.0 / math.sqrt(NOPE + ROPE_D)

    chosen = expert_ids[0]
    mask_own = jnp.sum(
        (chosen[:, :, None] == jnp.arange(expert_count)[None, None, :]).astype(F32), 1
    )
    mask_cols = tok * expert_count // rows
    pack_used = low_width + expert_count + 3
    pack = jnp.concatenate(
        [
            latent_down,
            router_weight,
            attn_gain[:, None],
            ffn_gain[:, None],
            jnp.pad(latent_gain, (0, rows - lat_rows))[:, None],
            mask_own.astype(BF).reshape(rows, mask_cols),
        ],
        1,
    )
    pack = pad_columns(pack, up_to(pack_used + mask_cols, 128))
    pack_full = gather_exp(by_part([pack] + [hop(pack, j) for j in range(1, 4)]))
    group_in = gather_ctx(inputs[0])
    weight_down = pack_full[:, :low_width]
    weight_router = pack_full[:, low_width : low_width + expert_count]
    gain_attn = pack_full[:, low_width + expert_count].astype(F32)
    gain_ffn = pack_full[:, low_width + expert_count + 1].astype(F32)
    gain_latent = (
        pack_full[:, low_width + expert_count + 2]
        .reshape(devices, rows)[:, :lat_rows]
        .reshape(KVR)
        .astype(F32)
    )
    mask = pack_full[:, pack_used : pack_used + mask_cols].reshape(total, expert_count).astype(F32)

    weight_query = to_heads(split_query(query_weight, parts))
    weight_up = to_heads(split_up(latent_up, parts))
    weight_output = lax.all_gather(output_weight, EXP, axis=0, tiled=True)
    own_shared = lax.all_to_all(
        jnp.concatenate(
            [w.reshape(rows, devices, 1, -1) for w in (shared_gate, shared_up)], 2
        ).reshape(rows, -1),
        ALL, split_axis=1, concat_axis=0, tiled=True,
    )
    own_sgate, own_sup = jnp.split(own_shared, 2, axis=1)
    chunks = max(1, total // 4096)

    early = chunks == 1 and lax.axis_size("chip") == 4

    group_rows = jnp.arange(group)
    place = place_of(my_part ^ (group_rows // tok), group_rows % tok, P_DEV * parts)
    allowed = place[None, :] <= place[:, None]
    cosine, sine = rotation(place, ROPE_D)
    cos_heads = jnp.tile(cosine, (1, own_heads))
    sin_heads = jnp.tile(sine, (1, own_heads))
    group_tokens = group_in.astype(F32)
    inv_root = lax.rsqrt(jnp.mean(group_tokens * group_tokens, -1, keepdims=True) + EPS)
    normed = (group_tokens * inv_root * gain_attn).astype(BF)
    if early:
        normed, cot_line = lax.optimization_barrier((normed, gather_line(cotangent[0])))
    query_raw = mm(normed, weight_query)
    wide = own_heads * NOPE
    narrow = own_heads * half
    query_nope = query_raw[:, :wide].astype(BF)
    query_first = query_raw[:, wide : wide + narrow]
    query_second = query_raw[:, wide + narrow :]
    turned_first = (query_first * cos_heads - query_second * sin_heads).astype(BF)
    turned_second = (query_first * sin_heads + query_second * cos_heads).astype(BF)
    query_rot = jnp.stack(
        [
            jnp.concatenate(
                [
                    query_nope[:, h * NOPE : (h + 1) * NOPE],
                    turned_first[:, h * half : (h + 1) * half],
                    turned_second[:, h * half : (h + 1) * half],
                ],
                1,
            )
            for h in range(own_heads)
        ]
    )
    latent_raw = mm(normed, weight_down)
    compressed = latent_raw[:, :KVR]
    latent_root = lax.rsqrt(jnp.mean(compressed * compressed, -1, keepdims=True) + EPS)
    latent_hat = compressed * latent_root
    latent_norm = (latent_hat * gain_latent).astype(BF)
    rope_first = latent_raw[:, KVR : KVR + half]
    rope_second = latent_raw[:, KVR + half :]
    key_rope = jnp.concatenate(
        [rope_first * cosine - rope_second * sine, rope_first * sine + rope_second * cosine], 1
    ).astype(BF)
    key_value = mm(latent_norm, weight_up).astype(BF)
    keys = jnp.stack(
        [
            jnp.concatenate([key_value[:, h * NOPE : (h + 1) * NOPE], key_rope], 1)
            for h in range(own_heads)
        ]
    )
    values = jnp.stack(
        [key_value[:, wide + h * VD : wide + (h + 1) * VD] for h in range(own_heads)]
    )
    scores = jnp.einsum("htd,hsd->hts", query_rot, keys, preferred_element_type=F32) * attn_scale
    scores = jnp.where(allowed[None], scores, -1e30)
    exp_scores = jnp.exp(scores - jnp.max(scores, -1, keepdims=True))
    probs = exp_scores / jnp.sum(exp_scores, -1, keepdims=True)
    weights_low = probs.astype(BF)
    attended = (
        jnp.einsum("hts,hsd->thd", weights_low, values, preferred_element_type=F32)
        .astype(BF)
        .reshape(group, own_heads * VD)
    )
    if early:
        attended, cot_pieces = lax.optimization_barrier((attended, gather_plane(cot_line)))
    projected = scatter_ctx(mm(attended, weight_output).astype(BF))
    tokens = inputs[0].astype(F32)
    hidden = tokens + projected
    inv_mid = lax.rsqrt(jnp.mean(hidden * hidden, -1, keepdims=True) + EPS)
    hidden_hat = hidden * inv_mid
    mixed = (hidden_hat * gain_ffn).astype(BF)

    exp_local, _, ff_own = expert_gate.shape
    routed = exp_local * ff_own
    own_units = routed + own_sgate.shape[1]
    weight_in = jnp.concatenate(
        [expert_gate[i] for i in range(exp_local)]
        + [own_sgate]
        + [expert_up[i] for i in range(exp_local)]
        + [own_sup, weight_router],
        1,
    )
    weight_out = jnp.concatenate([expert_down.reshape(routed, width), shared_down], 0)
    carried = up_to(expert_count, 128)
    weight_back = jnp.concatenate(
        [
            jnp.pad(weight_in[:, : 2 * own_units], ((0, 0), (0, carried))),
            jnp.pad(jnp.eye(carried, dtype=BF), ((0, 0), (2 * own_units, 0))),
        ],
        0,
    )
    first_expert = my_expert * exp_local

    def run_units(all_mixed, all_cot, mask):
        count = all_mixed.shape[0]
        activations = mm(all_mixed, weight_in)
        gate_activation = activations[:, :own_units]
        up_activation = activations[:, own_units : 2 * own_units]
        probs_all = jax.nn.softmax(activations[:, 2 * own_units :], axis=-1)
        gates_local = lax.dynamic_slice(probs_all * mask, (0, first_expert), (count, exp_local))
        mask_local = lax.dynamic_slice(mask, (0, first_expert), (count, exp_local))
        gate_columns = jnp.concatenate(
            [jnp.broadcast_to(gates_local[:, i : i + 1], (count, ff_own)) for i in range(exp_local)]
            + [jnp.ones((count, own_units - routed), F32)],
            1,
        )
        sigma = jax.nn.sigmoid(gate_activation)
        gated = gate_activation * sigma
        unit = (gated * up_activation).astype(BF).astype(F32)
        scaled_unit = (unit * gate_columns).astype(BF)
        grad_unit_raw = mm_nt(all_cot, weight_out)
        grad_gate_terms = grad_unit_raw * unit
        grad_gates = (
            jnp.concatenate(
                [
                    jnp.sum(grad_gate_terms[:, i * ff_own : (i + 1) * ff_own], 1, keepdims=True)
                    for i in range(exp_local)
                ],
                1,
            )
            * mask_local
        )
        grad_probs_part = lax.dynamic_update_slice(
            jnp.zeros((count, carried), F32), grad_gates, (0, first_expert)
        ).astype(BF)
        grad_unit = grad_unit_raw * gate_columns
        grad_gate_act = (
            grad_unit * up_activation * sigma * (1.0 + gate_activation * (1.0 - sigma))
        ).astype(BF)
        grad_up_act = (grad_unit * gated).astype(BF)
        grad_acts = jnp.concatenate([grad_gate_act, grad_up_act, grad_probs_part], 1)
        grad_mixed_part = mm_nt(grad_acts, weight_back).astype(BF)
        line = lax.axis_size("chip") == 4
        if line:
            grad_mixed_part, scaled_unit = lax.optimization_barrier((grad_mixed_part, scaled_unit))
            sums = scatter_cores(grad_mixed_part)
        out_part = mm(scaled_unit, weight_out).astype(BF)
        if line:
            sums, out_part, all_mixed, all_cot = lax.optimization_barrier(
                (sums, out_part, all_mixed, all_cot)
            )
        pair_grads = tuple(
            mm_tn(all_mixed, grad[:, i * ff_own : (i + 1) * ff_own])
            for grad in (grad_gate_act, grad_up_act)
            for i in range(exp_local)
        )
        routed_grads = (
            pair_grads,
            mm_tn(scaled_unit[:, :routed], all_cot),
            mm_tn(scaled_unit[:, routed:], all_cot),
        )
        shared_grads = mm_tn(
            all_mixed, jnp.concatenate([grad_gate_act[:, routed:], grad_up_act[:, routed:]], 1)
        ).astype(BF)
        if line:
            out_sums = scatter_cores(out_part)
            back, (out_sums, routed_grads, shared_grads) = scatter_rest(
                sums, (out_sums, routed_grads, shared_grads)
            )
            out_sum, _ = scatter_rest(out_sums, ())
        else:
            back = scatter_all(grad_mixed_part).astype(F32)
            out_sum = scatter_all(out_part)
        weight_grads = (*routed_grads, shared_grads)
        return out_sum, back, weight_grads

    mask_tokens = mask.reshape(devices, tok, expert_count)
    runs = []
    for i in range(chunks):
        span = slice(i * tok // chunks, (i + 1) * tok // chunks)
        own_mixed, own_cot = mixed[span], cotangent[0, span]
        if runs:
            own_mixed, own_cot, _ = lax.optimization_barrier((own_mixed, own_cot, runs[-1][:2]))
        runs.append(
            run_units(
                gather_all(own_mixed),
                gather_cores(cot_pieces) if early else gather_all(own_cot),
                mask_tokens[:, span].reshape(-1, expert_count),
            )
        )
    out_sum = jnp.concatenate([r[0] for r in runs], 0).astype(F32)
    back = jnp.concatenate([r[1] for r in runs], 0)
    pair_grads, grad_down, sum_sdown, grad_shared = jax.tree.map(
        lambda *terms: sum(terms[1:], terms[0].astype(F32)), *[r[2] for r in runs]
    )
    expert_gate_total = jnp.stack(pair_grads[:exp_local])
    expert_up_total = jnp.stack(pair_grads[exp_local:])
    expert_down_total = grad_down.reshape(exp_local, ff_own, width)
    sum_shared = lax.all_to_all(
        grad_shared.astype(BF).reshape(devices, rows, -1), ALL, split_axis=0, concat_axis=0,
        tiled=True,
    )
    sum_sgate, sum_sup = (
        part.transpose(1, 0, 2).reshape(rows, -1).astype(F32)
        for part in jnp.split(sum_shared, 2, axis=2)
    )

    grad_probs = back[:, width : width + expert_count]
    router_probs = jax.nn.softmax(mm(mixed, weight_router), axis=-1)
    grad_logits = (
        router_probs * (grad_probs - jnp.sum(router_probs * grad_probs, -1, keepdims=True))
    ).astype(BF)
    grad_router = mm_tn(mixed, grad_logits)
    grad_mixed = back[:, :width] + mm_nt(grad_logits, weight_router)
    grad_mid, grad_gain_ffn = norm_back(grad_mixed, hidden_hat, inv_mid, gain_ffn)
    grad_hidden = cotangent[0].astype(F32) + grad_mid
    grad_proj = gather_ctx(grad_hidden.astype(BF))
    grad_output = mm_tn(attended, grad_proj).astype(BF)
    grad_att = mm_nt(grad_proj, weight_output).astype(BF)
    grad_att = jnp.stack([grad_att[:, h * VD : (h + 1) * VD] for h in range(own_heads)])
    grad_weights = jnp.einsum("htd,hsd->hts", grad_att, values, preferred_element_type=F32)
    grad_values = jnp.einsum("hts,htd->shd", weights_low, grad_att, preferred_element_type=F32)
    grad_scores = (
        probs * (grad_weights - jnp.sum(probs * grad_weights, -1, keepdims=True))
    ).astype(BF)
    grad_query = (
        jnp.einsum("hts,hsd->htd", grad_scores, keys, preferred_element_type=F32) * attn_scale
    )
    grad_keys = (
        jnp.einsum("hts,htd->hsd", grad_scores, query_rot, preferred_element_type=F32) * attn_scale
    )
    grad_first = jnp.concatenate(
        [grad_query[h, :, NOPE : NOPE + half] for h in range(own_heads)], 1
    )
    grad_second = jnp.concatenate([grad_query[h, :, NOPE + half :] for h in range(own_heads)], 1)
    grad_qraw = jnp.concatenate(
        [grad_query[h, :, :NOPE] for h in range(own_heads)]
        + [
            grad_first * cos_heads + grad_second * sin_heads,
            grad_second * cos_heads - grad_first * sin_heads,
        ],
        1,
    ).astype(BF)
    grad_kv = jnp.concatenate(
        [grad_keys[h, :, :NOPE] for h in range(own_heads)]
        + [grad_values.reshape(group, own_heads * VD)],
        1,
    ).astype(BF)
    grad_low = jnp.concatenate(
        [mm_nt(grad_kv, weight_up), jnp.sum(grad_keys[:, :, NOPE:], 0)], 1
    )
    grad_low = scatter_ctx(pad_columns(grad_low.astype(BF), up_to(low_width, 128)))
    grad_front = scatter_ctx(mm_nt(grad_qraw, weight_query).astype(BF))
    head_grads = (mm_tn(normed, grad_qraw).astype(BF), mm_tn(latent_norm, grad_kv).astype(BF))
    sum_output = lax.psum_scatter(
        grad_output, EXP, scatter_dimension=0, tiled=True
    ).astype(F32)
    sum_query = join_query(from_heads(head_grads[0], parts), parts).astype(F32)
    sum_up = join_up(from_heads(head_grads[1], parts), parts).astype(F32)

    def own(values):
        return values[:tok]

    cos_own, sin_own = own(cosine), own(sine)
    grad_comp, grad_gain_latent = norm_back(
        grad_low[:, :KVR], own(latent_hat), own(latent_root), gain_latent
    )
    rope_grad_first = grad_low[:, KVR : KVR + half]
    rope_grad_second = grad_low[:, KVR + half : low_width]
    grad_lraw = jnp.concatenate(
        [
            grad_comp,
            rope_grad_first * cos_own + rope_grad_second * sin_own,
            rope_grad_second * cos_own - rope_grad_first * sin_own,
        ],
        1,
    ).astype(BF)
    lraw_group = gather_ctx(pad_columns(grad_lraw, up_to(low_width, 128)))[:, :low_width]
    block_rows = width // parts
    normed_block = lax.dynamic_slice_in_dim(normed, my_part * block_rows, block_rows, 1)
    grad_down = mm_tn(normed_block, lraw_group)
    grad_normed = grad_front + mm_nt(grad_lraw, weight_down)
    inv_own = own(inv_root)
    grad_entry, grad_gain_attn = norm_back(grad_normed, tokens * inv_own, inv_own, gain_attn)
    grad_inputs = grad_hidden + grad_entry

    small = jnp.concatenate(
        [
            grad_router,
            grad_gain_attn[:, None],
            grad_gain_ffn[:, None],
            jnp.pad(
                grad_gain_latent.reshape(devices, lat_rows), ((0, 0), (0, rows - lat_rows))
            ).reshape(width, 1),
        ],
        1,
    )
    small = pad_columns(small, up_to(pack_used, 128) - low_width).reshape(parts, block_rows, -1)
    small = by_part([small[a] for a in range(parts)])
    small = small[0] + sum(hop(small[j].astype(BF), j).astype(F32) for j in range(1, parts))
    pack_sum = scatter_exp(jnp.concatenate([grad_down, small], 1).astype(BF))
    return (
        (hidden + out_sum).astype(BF)[None],
        grad_inputs[None],
        pack_sum[:, low_width + expert_count],
        sum_query,
        pack_sum[:, :low_width],
        pack_sum[:lat_rows, low_width + expert_count + 2],
        sum_up,
        sum_output,
        pack_sum[:, low_width + expert_count + 1],
        pack_sum[:, low_width : low_width + expert_count],
        sum_sgate,
        sum_sup,
        sum_sdown,
        expert_gate_total,
        expert_up_total,
        expert_down_total,
    )


def solution(mesh):
    context, experts = mesh.devices.shape
    split = Mesh(mesh.devices.reshape(context, experts // 2, 2), ALL)
    tokens = P(EXP, CTX, None)
    dense = P(ALL, None)
    gain = P(ALL)
    columns = P(EXP, None, CTX)
    down = P(EXP, CTX, None)
    in_specs = (
        tokens, tokens, tokens, gain, dense, dense, gain, dense, dense, gain, dense, dense, dense,
        dense, columns, columns, down,
    )
    out_specs = (
        tokens, tokens, gain, dense, dense, gain, dense, dense, gain, dense, dense, dense, dense,
        columns, columns, down,
    )
    return jax.shard_map(
        shards, mesh=split, in_specs=in_specs, out_specs=out_specs, check_vma=False
    )
```
